32 devices in a mesh: rep: 8 (over z, x), space: 4 (over y, core).
Axes of the slice: x: 2, y: 2, z: 4, core: 2. Of those that a mesh axis runs over, the one named last changes fastest.
Arguments:
- positions: float32 [8, 3, 8, 4, 4, 128], P('rep', None, 'space'), may hold values from 0 to 1
- velocities: float32 [8, 3, 8, 4, 4, 128], P('rep', None, 'space'), may hold values from -12 to 12
- thermal_noise: float32 [8, 1, 3, 8, 4, 4, 128], P('rep', None, None, 'space'), may hold values from -6 to 6
- counts: int32 [8, 4, 4], P('space'), may hold values from 64 to 128, as said below
- pair_flags: int32 [13, 8, 4, 4], P(None, 'space'), may hold values 0 or 1
- exit_replica: int32 [8], replicated, may hold values from 0 to 7, each once
Outputs:
- quench_pos: float32 [8, 3, 8, 4, 4, 128], P('rep', None, 'space')
- quench_vel: float32 [8, 3, 8, 4, 4, 128], P('rep', None, 'space')
- dephase_pos: float32 [8, 3, 8, 4, 4, 128], P('rep', None, 'space')
- dephase_vel: float32 [8, 3, 8, 4, 4, 128], P('rep', None, 'space')
The draws below stay inside these ranges and needn't reach their ends.
Inputs may be any that keep to these rules, and one draw needn't show every extreme that they name: `counts`: the cell with the lowest indices of every aligned slab of 2 planes along the first dimension holds 128 atoms. `exit_replica`: every replica appears exactly once.
All inputs are finite; a program needn't handle non-finite values. No bound on the sum of `pair_flags` on one device may be relied on, other than what follows from the above.
Results may differ from the reference program's by a relative error of at most 0.0003.
Values sent between devices are 32-bit elements; how exact they have to be, the bound alone decides.
No kernel may reach another device: no remote copies, remote signals or barrier semaphores. Data moves between devices by JAX's collectives and lax.ppermute only.
A program may use at most 128 MiB of HBM per device.

```python
import math
import jax
import jax.numpy as jnp
from jax import lax

SLOTS = 128
CX_DEV = 2
GY = 4
GZ = 4
HALF = 13
QUENCH = 2
DEPHASE = 1
REPS = 8
NX = 8


def draw_velocities(key, part):
    base = jax.random.normal(key, (REPS, 3, NX, GY, GZ, SLOTS), jnp.float32)
    ramp = 1.0 + 2.0 * jnp.arange(NX, dtype=jnp.float32) / NX
    ramp_full = ramp[None, None, :, None, None, None]
    return jnp.clip(base * ramp_full, -12.0, 12.0)


def draw_counts(key, part):
    raw = jax.random.randint(key, (NX, GY, GZ), SLOTS // 2, SLOTS + 1)
    plane = lax_free_iota(NX, 0)
    row = lax_free_iota(GY, 1)
    col = lax_free_iota(GZ, 2)
    first = (plane % CX_DEV == 0) & (row == 0) & (col == 0)
    return jnp.where(first, SLOTS, raw).astype(jnp.int32)


def lax_free_iota(length, where):
    shape = [1, 1, 1]
    shape[where] = length
    return jnp.arange(length, dtype=jnp.int32).reshape(shape)


def plant(drawn, stream_key, low, high):
    shape = drawn.shape
    spot = [jax.random.randint(jax.random.fold_in(stream_key, axis), (), 0, shape[axis]) for axis in range(len(shape))]
    drawn = drawn.at[tuple(spot)].set(low)
    longest = shape.index(max(shape))
    spot[longest] = (spot[longest] + 1) % shape[longest]
    return drawn.at[tuple(spot)].set(high)


def block_levels(key, dims, shards, least, largest):
    def one(axis_at, blocks):
        steps = jax.random.uniform(jax.random.fold_in(jax.random.fold_in(key, 6), axis_at), (blocks,), jnp.float32, least / len(shards), largest / len(shards))
        return jnp.repeat(jnp.exp(steps), dims[axis_at] // blocks).reshape((-1,) + (1,) * (len(dims) - axis_at - 1))

    loudness = one(*shards[0])
    for cut in shards[1:]:
        loudness = loudness * one(*cut)
    return loudness


def centred(key, extent, scale, limit, cuts=(), kind=jnp.bfloat16):
    values = scale * jax.random.normal(key, extent, jnp.float32)
    if cuts:
        values = values * block_levels(key, extent, cuts, -0.22, 0.18)
    return jnp.clip(values, -limit, limit).astype(kind)


def setup_inputs(seed: int = 0) -> dict:
    arg_keys = jax.random.split(jax.random.key(seed), 7)
    positions = jnp.clip(1.0 * jax.random.uniform(arg_keys[0], (REPS, 3, NX, GY, GZ, SLOTS), jnp.float32) ** block_levels(arg_keys[0], (REPS, 3, NX, GY, GZ, SLOTS), ((0, 8), (2, 4)), -0.2, 0.2), 0.0, 1.0)
    velocities = draw_velocities(jax.random.fold_in(arg_keys[6], 71), 0)
    thermal_noise = centred(arg_keys[2], (REPS, DEPHASE, 3, NX, GY, GZ, SLOTS), 1.0, 6.0, ((0, 8), (3, 4)), jnp.float32)
    counts = draw_counts(jax.random.fold_in(arg_keys[6], 71), 0)
    pair_flags = plant((jax.random.randint(arg_keys[4], (HALF, NX, GY, GZ), 0, 4) < 3).astype(jnp.int32), jax.random.fold_in(arg_keys[4], 1), 0, 1)
    exit_replica = jax.random.permutation(arg_keys[5], REPS).astype(jnp.int32)
    return {"positions": positions, "velocities": velocities, "thermal_noise": thermal_noise, "counts": counts, "pair_flags": pair_flags, "exit_replica": exit_replica}


CUTOFF_SQ = 1.0
PAIR_A = 3.0
STEP_SIZE = 0.1
ALPHA_MIX = 0.25
EPSILON = 1e-06
FRICTION = math.exp(-0.2)
KICK_SCALE = math.sqrt(1.0 - FRICTION * FRICTION)
HALF_OFFSETS = [(1, p, q) for p in (-1, 0, 1) for q in (-1, 0, 1)] + [(0, 1, q) for q in (-1, 0, 1)] + [(0, 0, 1)]

def flag_lookup(ox, oy, oz):
    for index, entry in enumerate(HALF_OFFSETS):
        if entry == (ox, oy, oz):
            return (index, True)
        if entry == (-ox, -oy, -oz):
            return (index, False)
    return (0, True)

def plane_pass(pos_win, occ_win, flag_win, embed_win):
    slot_count = pos_win.shape[-1]
    center = pos_win[:, 1]
    occ_self = occ_win[1]
    diagonal = 1.0 - jnp.eye(slot_count, dtype=jnp.float32)
    if embed_win is None:
        result = jnp.zeros(occ_self.shape, jnp.float32)
    else:
        result = jnp.zeros(center.shape, jnp.float32)
        embed_self = embed_win[1]
    for ox in (-1, 0, 1):
        for oy in (-1, 0, 1):
            for oz in (-1, 0, 1):
                moved = (-oy, -oz)
                partner = jnp.roll(pos_win[:, 1 + ox], moved, axis=(1, 2))
                lattice = jnp.array([ox, oy, oz], dtype=jnp.float32)[:, None, None, None, None]
                displace = center[..., :, None] - partner[..., None, :] - lattice
                squared = lax.optimization_barrier(jnp.sum(displace * displace, axis=0))
                occ_peer = jnp.roll(occ_win[1 + ox], moved, axis=(0, 1))
                weight = occ_self[..., :, None] * occ_peer[..., None, :]
                if ox == 0 and oy == 0 and (oz == 0):
                    weight = weight * diagonal
                else:
                    index, forward = flag_lookup(ox, oy, oz)
                    if forward:
                        flag = flag_win[index, 1]
                    else:
                        flag = jnp.roll(flag_win[index, 1 + ox], moved, axis=(0, 1))
                    weight = weight * flag[..., None, None]
                closeness = jnp.maximum(1.0 - squared / CUTOFF_SQ, 0.0)
                if embed_win is None:
                    result = result + lax.optimization_barrier(jnp.sum(weight * closeness * closeness * closeness, axis=-1)) / slot_count
                else:
                    embed_peer = jnp.roll(embed_win[1 + ox], moved, axis=(0, 1))
                    slope = weight * (-4.0 * PAIR_A * closeness * closeness * closeness - 3.0 * (embed_self[..., :, None] + embed_peer[..., None, :]) * closeness * closeness) / slot_count
                    result = result - 2.0 * lax.optimization_barrier(jnp.sum(slope[None] * displace, axis=-1))
    return result

def blocked(pos_win, occ_win, flag_win, embed_win):
    planes = pos_win.shape[1] - 2

    def one_plane(index):
        part_pos = lax.dynamic_slice_in_dim(pos_win, index, 3, 1)
        part_occ = lax.dynamic_slice_in_dim(occ_win, index, 3, 0)
        part_flag = lax.dynamic_slice_in_dim(flag_win, index, 3, 1)
        part_embed = None if embed_win is None else lax.dynamic_slice_in_dim(embed_win, index, 3, 0)
        return plane_pass(part_pos, part_occ, part_flag, part_embed)
    stacked = lax.map(one_plane, jnp.arange(planes, dtype=jnp.int32))
    if embed_win is None:
        return stacked
    return jnp.moveaxis(stacked, 0, 1)

def periodic(array, width, axis_cells):
    total = array.shape[axis_cells]
    head = lax.slice_in_dim(array, total - width, total, axis=axis_cells)
    tail = lax.slice_in_dim(array, 0, width, axis=axis_cells)
    return jnp.concatenate([head, array, tail], axis=axis_cells)

def force_of(coords, occupied, flag_float):
    pos_pad = periodic(coords, 1, 1)
    occ_pad = periodic(occupied, 1, 0)
    flag_pad = periodic(flag_float, 1, 1)
    density = blocked(pos_pad, occ_pad, flag_pad, None)
    embed = -1.0 / jnp.sqrt(1.0 + density)
    return blocked(pos_pad, occ_pad, flag_pad, periodic(embed, 1, 0))

def reference(positions, velocities, thermal_noise, counts, pair_flags, exit_replica):
    slot_count = positions.shape[-1]
    occupied = (jnp.arange(slot_count, dtype=jnp.int32) < counts[..., None]).astype(jnp.float32)
    flag_float = pair_flags.astype(jnp.float32)

    def quench(pair):
        coords = pair[0]
        motion = pair[1] * occupied[None]
        for quench_step in range(QUENCH):
            forces = force_of(coords, occupied, flag_float)
            motion = motion + STEP_SIZE * forces
            mixing = jnp.sqrt(jnp.sum(motion * motion) / (jnp.sum(forces * forces) + EPSILON))
            motion = (1.0 - ALPHA_MIX) * motion + ALPHA_MIX * mixing * forces
            coords = coords + STEP_SIZE * motion
        return (coords, motion)
    quench_pos, quench_vel = lax.map(quench, (positions, velocities))
    chosen = exit_replica[0]
    exit_pos = lax.dynamic_index_in_dim(positions, chosen, 0, keepdims=False)
    exit_vel = lax.dynamic_index_in_dim(velocities, chosen, 0, keepdims=False) * occupied[None]
    exit_force = force_of(exit_pos, occupied, flag_float)

    def dephase(noise_rep):
        coords, motion, forces = (exit_pos, exit_vel, exit_force)
        for dephase_step in range(DEPHASE):
            if dephase_step > 0:
                forces = force_of(coords, occupied, flag_float)
            motion = motion + STEP_SIZE * forces
            motion = FRICTION * motion + KICK_SCALE * occupied[None] * noise_rep[dephase_step]
            coords = coords + STEP_SIZE * motion
        return (coords, motion)
    dephase_pos, dephase_vel = lax.map(dephase, thermal_noise)
    return (quench_pos, quench_vel, dephase_pos, dephase_vel)
```

```python
import functools
import math

import jax
import jax.numpy as jnp
from jax import lax
from jax.experimental import pallas as pl
from jax.experimental.pallas import tpu as pltpu
from jax.sharding import PartitionSpec as P

QUENCH = 2
STEP_SIZE = 0.1
ALPHA_MIX = 0.25
EPSILON = 1e-06
FRICTION = math.exp(-0.2)
KICK_SCALE = math.sqrt(1.0 - FRICTION * FRICTION)
HALF_OFFSETS = (
    [(1, p, q) for p in (-1, 0, 1) for q in (-1, 0, 1)]
    + [(0, 1, q) for q in (-1, 0, 1)]
    + [(0, 0, 1)]
)
OFFSETS = [(i, j, k) for i in (-1, 0, 1) for j in (-1, 0, 1) for k in (-1, 0, 1)]
FAR = 1.0e6
BF = jnp.bfloat16
F32 = jnp.float32
KDIM = 64


def ring(axis, shift):
    count = lax.axis_size(axis)
    return [(i, (i + shift) % count) for i in range(count)]


def flag_of(offset):
    for index, entry in enumerate(HALF_OFFSETS):
        if entry == offset:
            return index, True
        if entry == tuple(-v for v in offset):
            return index, False
    return None


def split3(value):
    high = value.astype(BF).astype(F32)
    rest = value - high
    mid = rest.astype(BF).astype(F32)
    return high, mid, (rest - mid).astype(BF).astype(F32)


def wrap(index, size):
    index = jnp.where(index < 0, index + size, index)
    return jnp.where(index >= size, index - size, index)


def build_list(dims, cnt_dummy, flags, flags_lo, list_ref):
    planes, gy, gz = dims
    ey, ez = gy + 2, gz + 2
    dummy = (planes + 2) * ey * ez

    def row(y, _):
        for p in range(planes):
            for z in range(gz):
                cell = (p * gy + y) * gz + z
                for slot, (ox, oy, oz) in enumerate(OFFSETS):
                    ext = ((p + 1 + ox) * ey + (y + 1 + oy)) * ez + (z + 1 + oz)
                    found = flag_of((ox, oy, oz))
                    if found is None:
                        list_ref[cell * 27 + slot] = ext
                        continue
                    index, forward = found
                    if forward:
                        flag = flags[index, p, y, z]
                    else:
                        jy, jz = wrap(y + oy, gy), (z + oz) % gz
                        if p + ox < 0:
                            flag = flags_lo[index, 0, jy, jz]
                        else:
                            flag = flags[index, p + ox, jy, jz]
                    list_ref[cell * 27 + slot] = jnp.where(flag > 0, ext, dummy)
        return 0

    lax.fori_loop(0, gy, row, 0)


def build_partners(dims, pos, cnt, emb, lhs_ref, yb_ref, sel_ref):
    planes, gy, gz = dims
    ey, ez = gy + 2, gz + 2
    slots = lhs_ref.shape[1]
    rows = lax.broadcasted_iota(jnp.int32, (8, slots), 0)
    lane = lax.broadcasted_iota(jnp.int32, (8, slots), 1)

    def one(j, which, at, y, z, by, bz):
        full = (8, slots)
        raw = [
            jnp.broadcast_to(pos[which][k, at, by, pl.ds(bz, 1), :], full) for k in range(3)
        ]
        xx = raw[0] + (j - 0.5 - (planes + 1) / 2)
        yy = raw[1] + ((y - 0.5 - (gy + 1) / 2) if isinstance(y, int) else (y.astype(F32) - 0.5 - (gy + 1) / 2))
        zz = raw[2] + (z - 0.5 - (gz + 1) / 2)
        norm = xx * xx + yy * yy + zz * zz
        norm = jnp.where(lane < cnt[which][at, by, bz], norm, norm + FAR)
        value = jnp.where(rows == 0, xx, jnp.where(rows == 1, yy, zz))
        value = jnp.where(rows == 3, norm, value)
        value = jnp.where(rows >= 4, 1.0, value)
        if emb is not None:
            e = jnp.broadcast_to(emb[which][at, by, pl.ds(bz, 1), :], full) * 0.25
            value = jnp.where(rows == 6, e, value)
        h, m, l = split3(value)
        return jnp.concatenate([h, h, h, m, m, m, l, l], axis=0)

    for j in range(planes + 2):
        which, at = (0, 0) if j == 0 else ((2, 0) if j == planes + 1 else (1, j - 1))

        def line(y, _):
            by = wrap(y - 1, gy)
            for z in range(ez):
                bz = (z - 1) % gz
                tall = one(j, which, at, y, z, by, bz)
                ext = (j * ey + y) * ez + z
                lhs_ref[ext] = tall.T.astype(BF)
            return 0

        lax.fori_loop(0, ey, line, 0)
        if yb_ref is not None:

            def broad(y, _):
                for z in range(gz):
                    out = jnp.concatenate(
                        split3(
                            jnp.concatenate(
                                [pos[which][k, at, y, pl.ds(z, 1), :] for k in range(3)]
                                + [jnp.zeros((5, slots), F32)],
                                axis=0,
                            )
                        ),
                        axis=0,
                    )
                    tall = out.T.astype(BF)
                    wide = jnp.dot(tall, sel_ref[...], preferred_element_type=F32)
                    cell = (j * gy + y) * gz + z
                    for k in range(3):
                        yb_ref[cell, k] = wide[:, k * slots : (k + 1) * slots]
                return 0

            lax.fori_loop(0, gy, broad, 0)
    dummy = (planes + 2) * ey * ez
    value = jnp.where(rows == 3, FAR, jnp.where(rows >= 4, 1.0, 0.0))
    h, m, l = split3(value)
    lhs_ref[dummy] = jnp.concatenate([h, h, h, m, m, m, l, l], axis=0).T.astype(BF)


def build_center(dims, p, y, z, x3, count, e_row):
    planes, gy, gz = dims
    slots = x3[0].shape[-1]
    full = (8, slots)
    rows = lax.broadcasted_iota(jnp.int32, full, 0)
    lane = lax.broadcasted_iota(jnp.int32, full, 1)
    xx = jnp.broadcast_to(x3[0], full) + (p + 0.5 - (planes + 1) / 2)
    yy = jnp.broadcast_to(x3[1], full) + (y.astype(F32) + 0.5 - (gy + 1) / 2)
    zz = jnp.broadcast_to(x3[2], full) + (z.astype(F32) + 0.5 - (gz + 1) / 2)
    one = 1.0 - (xx * xx + yy * yy + zz * zz)
    one = jnp.where(lane < count, one, one - FAR)
    value = jnp.where(rows == 0, xx, jnp.where(rows == 1, yy, zz)) * 2.0
    value = jnp.where(rows == 4, one, value)
    if e_row is not None:
        value = jnp.where(rows == 5, jnp.broadcast_to(e_row, full) * 0.25, value)
    parts = split3(value)
    us, ws = [], []
    for block in range(8):
        part = parts[block % 3]
        keep = rows < 3
        if block < 3:
            keep = keep | (rows == 4)
        u = jnp.where(keep, part, 0.0)
        if block % 3 == 0:
            u = jnp.where(rows == 3, -1.0, u)
        us.append(u)
        if e_row is not None:
            w = u
            if block < 3:
                w = jnp.where(rows == 5, part, w)
            if block % 3 == 0:
                w = jnp.where(rows == 6, 1.0, w)
            ws.append(w)
    right = jnp.concatenate(us, axis=0).astype(BF)
    if e_row is None:
        return right
    return jnp.concatenate([right, jnp.concatenate(ws, axis=0).astype(BF)], axis=1)


def density_kernel(dims, first, *refs):
    if first:
        (p0, p1, p2, c0, c1, c2, fl, fl_lo, emb_ref, list_ref, lhs_ref) = refs
        build_list(dims, None, fl, fl_lo, list_ref)
    else:
        (p0, p1, p2, c0, c1, c2, list_ref, emb_ref, lhs_ref) = refs
    planes, gy, gz = dims
    slots = lhs_ref.shape[1]
    build_partners(dims, (p0, p1, p2), (c0, c1, c2), None, lhs_ref, None, None)
    lane = lax.broadcasted_iota(jnp.int32, (1, slots), 1)
    for p in range(planes):

        def cell_step(i, _):
            y, z = i // gz, i % gz
            x3 = [p1[k, p, y, pl.ds(z, 1), :] for k in range(3)]
            count = c1[p, y, z]
            right = build_center(dims, p, y, z, x3, count, None)
            cell = p * gy * gz + i
            acc = [jnp.zeros((8, slots), F32) for _ in range(4)]
            for slot in range(27):
                u = jnp.dot(lhs_ref[list_ref[cell * 27 + slot]], right, preferred_element_type=F32)
                for r in range(slots // 8):
                    t = jnp.maximum(u[r * 8 : r * 8 + 8], 0.0)
                    acc[r % 4] = acc[r % 4] + t * t * t
            total = jnp.sum((acc[0] + acc[1]) + (acc[2] + acc[3]), axis=0, keepdims=True)
            total = total - jnp.where(lane < count, 1.0, 0.0)
            emb_ref[p, y, pl.ds(z, 1), :] = -lax.rsqrt(1.0 + total / slots)
            return 0

        lax.fori_loop(0, gy * gz, cell_step, 0)


def force_kernel(dims, *refs):
    (p0, p1, p2, c0, c1, c2, e0, e1, e2, vel, list_ref, sel_ref, f_ref, v_ref, s_ref, lhs_ref, yb_ref) = refs
    planes, gy, gz = dims
    slots = lhs_ref.shape[1]
    build_partners(dims, (p0, p1, p2), (c0, c1, c2), (e0, e1, e2), lhs_ref, yb_ref, sel_ref)
    lane = lax.broadcasted_iota(jnp.int32, (1, slots), 1)
    sums = (jnp.zeros((1, slots), F32), jnp.zeros((1, slots), F32))
    for p in range(planes):

        def cell_step(i, sums):
            y, z = i // gz, i % gz
            x3 = [p1[k, p, y, pl.ds(z, 1), :] for k in range(3)]
            count = c1[p, y, z]
            right = build_center(dims, p, y, z, x3, count, e1[p, y, pl.ds(z, 1), :])
            cell = p * gy * gz + i
            zero = jnp.zeros((8, slots), F32)
            s0, s1, extra = zero, [zero] * 3, [zero] * 3
            for slot, offset in enumerate(OFFSETS):
                both = jnp.dot(lhs_ref[list_ref[cell * 27 + slot]], right, preferred_element_type=F32)
                base = ((p + 1 + offset[0]) * gy + wrap(y + offset[1], gy)) * gz + wrap(z + offset[2], gz)
                part = None
                for r in range(slots // 8):
                    here = slice(r * 8, r * 8 + 8)
                    t = jnp.maximum(both[here, :slots], 0.0)
                    g = t * t * both[here, slots:]
                    part = g if part is None else part + g
                    for k in range(3):
                        s1[k] = s1[k] + g * yb_ref[base, k, here, :]
                s0 = s0 + part
                for k in range(3):
                    if offset[k] == 1:
                        extra[k] = extra[k] + part
                    elif offset[k] == -1:
                        extra[k] = extra[k] - part
            total = jnp.sum(s0, axis=0, keepdims=True)
            ff, vv = sums
            for k in range(3):
                f = (24.0 / slots) * (
                    x3[k] * total - jnp.sum(s1[k] + extra[k], axis=0, keepdims=True)
                )
                f_ref[k, p, y, pl.ds(z, 1), :] = f
                v = jnp.where(lane < count, vel[k, p, y, pl.ds(z, 1), :], 0.0) + STEP_SIZE * f
                v_ref[k, p, y, pl.ds(z, 1), :] = v
                ff = ff + f * f
                vv = vv + v * v
            return ff, vv

        sums = lax.fori_loop(0, gy * gz, cell_step, sums)
    s_ref[...] = jnp.concatenate([sums[0], sums[1], jnp.zeros((6, slots), F32)], axis=0)


def body(positions, velocities, thermal_noise, counts, pair_flags, exit_replica):
    start_pos = positions[0]
    start_vel = velocities[0]
    planes, gy, gz, slots = start_pos.shape[1:]
    dims = (planes, gy, gz)
    up, down = ring("space", 1), ring("space", -1)
    vmem = pl.BlockSpec(memory_space=pltpu.VMEM)
    smem = pl.BlockSpec(memory_space=pltpu.SMEM)
    params = pltpu.CompilerParams(vmem_limit_bytes=56 * 2**20)
    ext = (planes + 2) * (gy + 2) * (gz + 2) + 1
    entries = planes * gy * gz * 27
    cells = planes * gy * gz
    pairs = cells * 27 * slots * slots

    def halo(block, dim):
        low = lax.ppermute(lax.slice_in_dim(block, planes - 1, planes, axis=dim), "space", up)
        high = lax.ppermute(lax.slice_in_dim(block, 0, 1, axis=dim), "space", down)
        return low, high

    count_lo, count_hi = halo(counts, 0)
    flags_lo = lax.ppermute(lax.slice_in_dim(pair_flags, planes - 1, planes, axis=1), "space", up)
    column = jnp.arange(24)[:, None]
    pick = ((column % 8) == (jnp.arange(3 * slots)[None, :] // slots)).astype(BF)
    lhs_scratch = pltpu.VMEM((ext, slots, KDIM), BF)
    emb_shape = jax.ShapeDtypeStruct((planes, gy, gz, slots), F32)
    vec_shape = jax.ShapeDtypeStruct((3, planes, gy, gz, slots), F32)

    coords, motion = start_pos, start_vel
    blocks = None
    pushed = None
    for quench_step in range(QUENCH):
        low, high = halo(coords, 1)
        args = [low, coords, high, count_lo, counts, count_hi]
        specs = [vmem] * 3 + [smem] * 3
        cost = pl.CostEstimate(flops=pairs * 10, bytes_accessed=2**20, transcendentals=0)
        if quench_step == 0:
            embed, blocks = pl.pallas_call(
                functools.partial(density_kernel, dims, True),
                out_shape=(emb_shape, jax.ShapeDtypeStruct((entries,), jnp.int32)),
                in_specs=specs + [smem, smem],
                out_specs=(vmem, smem),
                scratch_shapes=[lhs_scratch],
                compiler_params=params,
                cost_estimate=cost,
                name="density_first",
            )(*args, pair_flags, flags_lo)
        else:
            embed = pl.pallas_call(
                functools.partial(density_kernel, dims, False),
                out_shape=emb_shape,
                in_specs=specs + [smem],
                out_specs=vmem,
                scratch_shapes=[lhs_scratch],
                compiler_params=params,
                cost_estimate=cost,
                name="density_next",
            )(*args, blocks)
        embed_lo, embed_hi = halo(embed, 0)
        forces, pushed_vel, sums = pl.pallas_call(
            functools.partial(force_kernel, dims),
            out_shape=(vec_shape, vec_shape, jax.ShapeDtypeStruct((8, slots), F32)),
            in_specs=specs + [vmem] * 4 + [smem, vmem],
            out_specs=(vmem, vmem, vmem),
            scratch_shapes=[
                lhs_scratch,
                pltpu.VMEM(((planes + 2) * gy * gz, 3, slots, slots), F32),
            ],
            compiler_params=params,
            cost_estimate=pl.CostEstimate(
                flops=pairs * 25, bytes_accessed=2**20, transcendentals=0
            ),
            name="force",
        )(*args, embed_lo, embed, embed_hi, motion, blocks, pick)
        if quench_step == 0:
            pushed = pushed_vel
        total = sums
        for shift in range(1, lax.axis_size("space")):
            total = total + lax.ppermute(sums, "space", ring("space", shift))
        force_sq, vel_sq = jnp.sum(total[0]), jnp.sum(total[1])
        mixing = jnp.sqrt(vel_sq / (force_sq + EPSILON))
        motion = (1.0 - ALPHA_MIX) * pushed_vel + ALPHA_MIX * mixing * forces
        coords = coords + STEP_SIZE * motion

    chosen = exit_replica[0]
    held = jnp.concatenate([start_pos, pushed], axis=0)
    replicas = lax.axis_size("rep")
    me = lax.axis_index("rep")
    if replicas & (replicas - 1) == 0:
        stride = 1
        while stride < replicas:
            other = lax.ppermute(held, "rep", [(i, i ^ stride) for i in range(replicas)])
            mine = ((me ^ chosen) >> (stride.bit_length() - 1)) & 1 == 0
            held = jnp.where(mine, held, other)
            stride *= 2
    else:
        final = held
        for shift in range(1, replicas):
            other = lax.ppermute(held, "rep", ring("rep", shift))
            final = jnp.where((me - shift) % replicas == chosen, other, final)
        held = final
    exit_pos, exit_push = held[:3], held[3:]
    occupied = (jnp.arange(slots, dtype=jnp.int32) < counts[..., None]).astype(F32)
    drift = FRICTION * exit_push + KICK_SCALE * occupied[None] * thermal_noise[0, 0]
    place = exit_pos + STEP_SIZE * drift
    return coords[None], motion[None], place[None], drift[None]


def solution(mesh):
    vector = P("rep", None, "space", None, None, None)
    placed = (
        vector,
        vector,
        P("rep", None, None, "space", None, None, None),
        P("space", None, None),
        P(None, "space", None, None),
        P(),
    )
    return jax.shard_map(
        body, mesh=mesh, in_specs=placed, out_specs=(vector,) * 4, check_vma=False
    )
```

```python
import functools
import math

import jax
import jax.numpy as jnp
from jax import lax
from jax.experimental import pallas as pl
from jax.experimental.pallas import tpu as pltpu
from jax.sharding import PartitionSpec as P


QUENCH = 2
STEP_SIZE = 0.1
ALPHA_MIX = 0.25
EPSILON = 1e-06
FRICTION = math.exp(-0.2)
KICK_SCALE = math.sqrt(1.0 - FRICTION * FRICTION)
HALF_OFFSETS = (
    [(1, p, q) for p in (-1, 0, 1) for q in (-1, 0, 1)]
    + [(0, 1, q) for q in (-1, 0, 1)]
    + [(0, 0, 1)]
)
OFFSETS = [(i, j, k) for i in (-1, 0, 1) for j in (-1, 0, 1) for k in (-1, 0, 1)]
FAR = 1.0e6
BF = jnp.bfloat16
F32 = jnp.float32
KDIM = 64


def ring(axis, shift):
    count = lax.axis_size(axis)
    return [(i, (i + shift) % count) for i in range(count)]


def flag_of(offset):
    for index, entry in enumerate(HALF_OFFSETS):
        if entry == offset:
            return index, True
        if entry == tuple(-v for v in offset):
            return index, False
    return None


def split3(value):
    high = value.astype(BF).astype(F32)
    rest = value - high
    mid = rest.astype(BF).astype(F32)
    return high, mid, (rest - mid).astype(BF).astype(F32)


def wrap(index, size):
    index = jnp.where(index < 0, index + size, index)
    return jnp.where(index >= size, index - size, index)


def build_list(dims, flags, flags_lo, list_ref):
    planes, gy, gz = dims
    ey, ez = gy + 2, gz + 2
    dummy = (planes + 2) * ey * ez

    def row(y, _):
        for p in range(planes):
            for z in range(gz):
                cell = (p * gy + y) * gz + z
                for slot, (ox, oy, oz) in enumerate(OFFSETS):
                    ext = ((p + 1 + ox) * ey + (y + 1 + oy)) * ez + (z + 1 + oz)
                    found = flag_of((ox, oy, oz))
                    if found is None:
                        list_ref[cell * 27 + slot] = ext
                        continue
                    index, forward = found
                    if forward:
                        flag = flags[index, p, y, z]
                    else:
                        jy, jz = wrap(y + oy, gy), (z + oz) % gz
                        if p + ox < 0:
                            flag = flags_lo[index, 0, jy, jz]
                        else:
                            flag = flags[index, p + ox, jy, jz]
                    list_ref[cell * 27 + slot] = jnp.where(flag > 0, ext, dummy)
        return 0

    lax.fori_loop(0, gy, row, 0)


def build_partners(dims, pos, cnt, emb, lhs_ref, yb_ref):
    planes, gy, gz = dims
    ey, ez = gy + 2, gz + 2
    slots = lhs_ref.shape[1]
    rows = lax.broadcasted_iota(jnp.int32, (8, slots), 0)
    lane = lax.broadcasted_iota(jnp.int32, (8, slots), 1)

    def one(j, which, at, y, z, by, bz):
        full = (8, slots)
        raw = [
            jnp.broadcast_to(pos[which][k, at, by, pl.ds(bz, 1), :], full) for k in range(3)
        ]
        xx = raw[0] + (j - 0.5 - (planes + 1) / 2)
        yy = raw[1] + ((y - 0.5 - (gy + 1) / 2) if isinstance(y, int) else (y.astype(F32) - 0.5 - (gy + 1) / 2))
        zz = raw[2] + (z - 0.5 - (gz + 1) / 2)
        norm = xx * xx + yy * yy + zz * zz
        norm = jnp.where(lane < cnt[which][at, by, bz], norm, norm + FAR)
        value = jnp.where(rows == 0, xx, jnp.where(rows == 1, yy, zz))
        value = jnp.where(rows == 3, norm, value)
        value = jnp.where(rows >= 4, 1.0, value)
        if emb is not None:
            e = jnp.broadcast_to(emb[which][at, by, pl.ds(bz, 1), :], full) * 0.25
            value = jnp.where(rows == 6, e, value)
        h, m, l = split3(value)
        return jnp.concatenate([h, h, h, m, m, m, l, l], axis=0)

    for j in range(planes + 2):
        which, at = (0, 0) if j == 0 else ((2, 0) if j == planes + 1 else (1, j - 1))

        def line(y, _):
            by = wrap(y - 1, gy)
            for z in range(ez):
                bz = (z - 1) % gz
                tall = one(j, which, at, y, z, by, bz)
                ext = (j * ey + y) * ez + z
                lhs_ref[ext] = tall.T.astype(BF)
            return 0

        lax.fori_loop(0, ey, line, 0)
        if yb_ref is not None:
            col = lax.broadcasted_iota(jnp.int32, (24, 3 * slots), 0) % 8
            pick = (col == lax.broadcasted_iota(jnp.int32, (24, 3 * slots), 1) // slots).astype(F32).astype(BF)

            def broad(y, _):
                for z in range(gz):
                    out = jnp.concatenate(
                        split3(
                            jnp.concatenate(
                                [pos[which][k, at, y, pl.ds(z, 1), :] for k in range(3)]
                                + [jnp.zeros((5, slots), F32)],
                                axis=0,
                            )
                        ),
                        axis=0,
                    )
                    tall = out.T.astype(BF)
                    wide = jnp.dot(tall, pick, preferred_element_type=F32)
                    cell = (j * gy + y) * gz + z
                    for k in range(3):
                        yb_ref[cell, k] = wide[:, k * slots : (k + 1) * slots]
                return 0

            lax.fori_loop(0, gy, broad, 0)
    dummy = (planes + 2) * ey * ez
    value = jnp.where(rows == 3, FAR, jnp.where(rows >= 4, 1.0, 0.0))
    h, m, l = split3(value)
    lhs_ref[dummy] = jnp.concatenate([h, h, h, m, m, m, l, l], axis=0).T.astype(BF)


def build_center(dims, p, y, z, x3, count, e_row):
    planes, gy, gz = dims
    slots = x3[0].shape[-1]
    full = (8, slots)
    rows = lax.broadcasted_iota(jnp.int32, full, 0)
    lane = lax.broadcasted_iota(jnp.int32, full, 1)
    xx = jnp.broadcast_to(x3[0], full) + (p + 0.5 - (planes + 1) / 2)
    yy = jnp.broadcast_to(x3[1], full) + (y.astype(F32) + 0.5 - (gy + 1) / 2)
    zz = jnp.broadcast_to(x3[2], full) + (z.astype(F32) + 0.5 - (gz + 1) / 2)
    one = 1.0 - (xx * xx + yy * yy + zz * zz)
    one = jnp.where(lane < count, one, one - FAR)
    value = jnp.where(rows == 0, xx, jnp.where(rows == 1, yy, zz)) * 2.0
    value = jnp.where(rows == 4, one, value)
    if e_row is not None:
        value = jnp.where(rows == 5, jnp.broadcast_to(e_row, full) * 0.25, value)
    parts = split3(value)
    us, ws = [], []
    for block in range(8):
        part = parts[block % 3]
        keep = rows < 3
        if block < 3:
            keep = keep | (rows == 4)
        u = jnp.where(keep, part, 0.0)
        if block % 3 == 0:
            u = jnp.where(rows == 3, -1.0, u)
        us.append(u)
        if e_row is not None:
            w = u
            if block < 3:
                w = jnp.where(rows == 5, part, w)
            if block % 3 == 0:
                w = jnp.where(rows == 6, 1.0, w)
            ws.append(w)
    right = jnp.concatenate(us, axis=0).astype(BF)
    if e_row is None:
        return right
    return jnp.concatenate([right, jnp.concatenate(ws, axis=0).astype(BF)], axis=1)


def mix_factor(sum_refs):
    total = sum_refs[0][...]
    for ref in sum_refs[1:]:
        total = total + ref[...]
    force_sq = jnp.sum(total[0:1], axis=1, keepdims=True)
    vel_sq = jnp.sum(total[1:2], axis=1, keepdims=True)
    return jnp.sqrt(vel_sq / (force_sq + EPSILON))


def quench_update(dims, mix, x_ref, f_of, v_of, planes, x_out, v_out):
    gy, _ = dims[1:]
    for k in range(3):
        for p in range(planes):
            for y in range(gy):
                v = (1.0 - ALPHA_MIX) * v_of(k, p, y) + ALPHA_MIX * mix * f_of(k, p, y)
                if v_out is not None:
                    v_out[k, p, y] = v
                x_out[k, p, y] = x_ref[k, p, y] + STEP_SIZE * v


def density_kernel(dims, first, *refs):
    planes, gy, gz = dims
    if first:
        (p0, p1, p2, c0, c1, c2, fl, fl_lo, emb_ref, lo_ref, hi_ref, list_ref, lhs_ref) = refs
        build_list(dims, fl, fl_lo, list_ref)
    else:
        (q0, q1, q2, c0, c1, c2, list_ref, f_ref, v_ref, b0, b2) = refs[:11]
        sum_refs = refs[11:-8]
        (emb_ref, lo_ref, hi_ref, p0, p1, p2, v_out, lhs_ref) = refs[-8:]
        mix = mix_factor(sum_refs)
        quench_update(
            dims, mix, q1, lambda k, p, y: f_ref[k, p, y], lambda k, p, y: v_ref[k, p, y], planes, p1, v_out
        )
        for q, b, out in ((q0, b0, p0), (q2, b2, p2)):
            quench_update(
                dims, mix, q, lambda k, p, y, b=b: b[k, p, y], lambda k, p, y, b=b: b[k + 3, p, y], 1, out, None
            )
    slots = lhs_ref.shape[1]
    build_partners(dims, (p0, p1, p2), (c0, c1, c2), None, lhs_ref, None)
    lane = lax.broadcasted_iota(jnp.int32, (1, slots), 1)
    for p in range(planes):

        def cell_step(i, _):
            y, z = i // gz, i % gz
            x3 = [p1[k, p, y, pl.ds(z, 1), :] for k in range(3)]
            count = c1[p, y, z]
            right = build_center(dims, p, y, z, x3, count, None)
            cell = p * gy * gz + i
            acc = [jnp.zeros((8, slots), F32) for _ in range(4)]
            for slot in range(27):
                u = jnp.dot(lhs_ref[list_ref[cell * 27 + slot]], right, preferred_element_type=F32)
                for r in range(slots // 8):
                    t = jnp.maximum(u[r * 8 : r * 8 + 8], 0.0)
                    acc[r % 4] = acc[r % 4] + t * t * t
            total = jnp.sum((acc[0] + acc[1]) + (acc[2] + acc[3]), axis=0, keepdims=True)
            total = total - jnp.where(lane < count, 1.0, 0.0)
            emb = -lax.rsqrt(1.0 + total / slots)
            emb_ref[p, y, pl.ds(z, 1), :] = emb
            if p == 0:
                lo_ref[0, y, pl.ds(z, 1), :] = emb
            if p == planes - 1:
                hi_ref[0, y, pl.ds(z, 1), :] = emb
            return 0

        lax.fori_loop(0, gy * gz, cell_step, 0)


def force_kernel(dims, *refs):
    (p0, p1, p2, c0, c1, c2, e0, e1, e2, vel, list_ref) = refs[:11]
    (f_ref, v_ref, s_ref) = refs[11:14]
    edges = refs[14:-2]
    (lhs_ref, yb_ref) = refs[-2:]
    planes, gy, gz = dims
    slots = lhs_ref.shape[1]
    build_partners(dims, (p0, p1, p2), (c0, c1, c2), (e0, e1, e2), lhs_ref, yb_ref)
    lane = lax.broadcasted_iota(jnp.int32, (1, slots), 1)
    sums = (jnp.zeros((1, slots), F32), jnp.zeros((1, slots), F32))
    for p in range(planes):

        def cell_step(i, sums):
            y, z = i // gz, i % gz
            x3 = [p1[k, p, y, pl.ds(z, 1), :] for k in range(3)]
            count = c1[p, y, z]
            right = build_center(dims, p, y, z, x3, count, e1[p, y, pl.ds(z, 1), :])
            cell = p * gy * gz + i
            zero = jnp.zeros((8, slots), F32)
            s0, s1, extra = zero, [zero] * 3, [zero] * 3
            for slot, offset in enumerate(OFFSETS):
                both = jnp.dot(lhs_ref[list_ref[cell * 27 + slot]], right, preferred_element_type=F32)
                base = ((p + 1 + offset[0]) * gy + wrap(y + offset[1], gy)) * gz + wrap(z + offset[2], gz)
                part = None
                for r in range(slots // 8):
                    here = slice(r * 8, r * 8 + 8)
                    t = jnp.maximum(both[here, :slots], 0.0)
                    g = t * t * both[here, slots:]
                    part = g if part is None else part + g
                    for k in range(3):
                        s1[k] = s1[k] + g * yb_ref[base, k, here, :]
                s0 = s0 + part
                for k in range(3):
                    if offset[k] == 1:
                        extra[k] = extra[k] + part
                    elif offset[k] == -1:
                        extra[k] = extra[k] - part
            total = jnp.sum(s0, axis=0, keepdims=True)
            ff, vv = sums
            for k in range(3):
                f = (24.0 / slots) * (
                    x3[k] * total - jnp.sum(s1[k] + extra[k], axis=0, keepdims=True)
                )
                f_ref[k, p, y, pl.ds(z, 1), :] = f
                v = jnp.where(lane < count, vel[k, p, y, pl.ds(z, 1), :], 0.0) + STEP_SIZE * f
                v_ref[k, p, y, pl.ds(z, 1), :] = v
                if edges and p == 0:
                    edges[0][k, 0, y, pl.ds(z, 1), :] = f
                    edges[0][k + 3, 0, y, pl.ds(z, 1), :] = v
                if edges and p == planes - 1:
                    edges[1][k, 0, y, pl.ds(z, 1), :] = f
                    edges[1][k + 3, 0, y, pl.ds(z, 1), :] = v
                ff = ff + f * f
                vv = vv + v * v
            return ff, vv

        sums = lax.fori_loop(0, gy * gz, cell_step, sums)
    s_ref[...] = jnp.concatenate([sums[0], sums[1], jnp.zeros((6, slots), F32)], axis=0)


def finish_kernel(dims, radix, *refs):
    (x_ref, f_ref, v_ref, noise, cnt, pick) = refs[:6]
    options = refs[6 : 6 + radix]
    sum_refs = refs[6 + radix : -4]
    (xq, vq, xd, vd) = refs[-4:]
    planes, gy, gz = dims
    slots = x_ref.shape[-1]
    mix = mix_factor(sum_refs)
    quench_update(
        dims, mix, x_ref, lambda k, p, y: f_ref[k, p, y], lambda k, p, y: v_ref[k, p, y], planes, xq, vq
    )
    lane = lax.broadcasted_iota(jnp.int32, (gz, slots), 1)
    line = lax.broadcasted_iota(jnp.int32, (gz, slots), 0)
    take = pick[0]
    for p in range(planes):
        for y in range(gy):
            limit = jnp.zeros((gz, slots), jnp.int32)
            for z in range(gz):
                limit = jnp.where(line == z, cnt[p, y, z], limit)
            occupied = (lane < limit).astype(F32)
            for k in range(3):
                place, push = options[0][k, p, y], options[0][k + 3, p, y]
                for index in range(1, radix):
                    place = jnp.where(take == index, options[index][k, p, y], place)
                    push = jnp.where(take == index, options[index][k + 3, p, y], push)
                v = FRICTION * push + KICK_SCALE * occupied * noise[k, p, y]
                vd[k, p, y] = v
                xd[k, p, y] = place + STEP_SIZE * v


def exit_hops(count):
    hops, stride = [], 1
    while stride < count:
        left = count // stride
        radix = next(r for r in (4, 2, 3, 5, 7, left) if left % r == 0)
        hops.append((stride, radix))
        stride *= radix
    return hops


def body(positions, velocities, thermal_noise, counts, pair_flags, exit_replica):
    start_pos = positions[0]
    start_vel = velocities[0]
    planes, gy, gz, slots = start_pos.shape[1:]
    dims = (planes, gy, gz)
    up, down = ring("space", 1), ring("space", -1)
    space = lax.axis_size("space")
    vmem = pl.BlockSpec(memory_space=pltpu.VMEM)
    smem = pl.BlockSpec(memory_space=pltpu.SMEM)
    ext = (planes + 2) * (gy + 2) * (gz + 2) + 1
    entries = planes * gy * gz * 27
    pairs = planes * gy * gz * 27 * slots * slots

    def shaped(*shape):
        return jax.ShapeDtypeStruct(shape, F32)

    def planes_of(block, dim):
        return lax.slice_in_dim(block, 0, 1, axis=dim), lax.slice_in_dim(block, planes - 1, planes, axis=dim)

    def halo(first, last):
        return lax.ppermute(last, "space", up), lax.ppermute(first, "space", down)

    flags_lo = lax.ppermute(lax.slice_in_dim(pair_flags, planes - 1, planes, axis=1), "space", up)
    count_lo, count_hi = halo(*planes_of(counts, 0))
    pos_lo, pos_hi = halo(*planes_of(start_pos, 1))
    lhs_scratch = pltpu.VMEM((ext, slots, KDIM), BF)
    emb_shape = [shaped(planes, gy, gz, slots), shaped(1, gy, gz, slots), shaped(1, gy, gz, slots)]
    vec, edge = shaped(3, planes, gy, gz, slots), shaped(3, 1, gy, gz, slots)
    pack = shaped(6, 1, gy, gz, slots)
    number = [smem] * 3
    cost_d = pl.CostEstimate(flops=pairs * 10, bytes_accessed=2**20, transcendentals=0)
    cost_f = pl.CostEstimate(flops=pairs * 25, bytes_accessed=2**20, transcendentals=0)

    held, hops = None, exit_hops(lax.axis_size("rep"))
    me, chosen = lax.axis_index("rep"), exit_replica[0]

    def hop(index, held):
        stride, radix = hops[index]
        digit, root = (me // stride) % radix, (chosen // stride) % radix
        options = [held]
        for turn in range(1, radix):
            pairs = []
            for i in range(lax.axis_size("rep")):
                at = (i // stride) % radix
                pairs.append((i, i + (((at + turn) % radix) - at) * stride))
            options.append(lax.ppermute(held, "rep", pairs))
        return options, (digit - root) % radix

    motion = start_vel
    coords = (pos_lo, start_pos, pos_hi)
    for quench_step in range(QUENCH):
        args = [*coords, count_lo, counts, count_hi]
        specs = [vmem] * 3 + number
        if quench_step == 0:
            emb, emb_first, emb_last, blocks = pl.pallas_call(
                functools.partial(density_kernel, dims, True),
                out_shape=(*emb_shape, jax.ShapeDtypeStruct((entries,), jnp.int32)),
                in_specs=specs + [smem, smem],
                out_specs=(vmem, vmem, vmem, smem),
                scratch_shapes=[lhs_scratch],
                compiler_params=pltpu.CompilerParams(vmem_limit_bytes=12 * 2**20),
                cost_estimate=cost_d,
                name="density_first",
            )(*args, pair_flags, flags_lo)
        else:
            emb, emb_first, emb_last, *coords, motion = pl.pallas_call(
                functools.partial(density_kernel, dims, False),
                out_shape=(*emb_shape, edge, vec, edge, vec),
                in_specs=specs + [smem] + [vmem] * (4 + space),
                out_specs=(vmem,) * 7,
                scratch_shapes=[lhs_scratch],
                compiler_params=pltpu.CompilerParams(vmem_limit_bytes=12 * 2**20),
                cost_estimate=cost_d,
                name="density_next",
            )(*args, blocks, forces, pushed, *packs, *sums)
            args = [*coords, count_lo, counts, count_hi]
        emb_lo, emb_hi = halo(emb_first, emb_last)
        last = quench_step == QUENCH - 1
        forces, pushed, part, *edges = pl.pallas_call(
            functools.partial(force_kernel, dims),
            out_shape=(vec, vec, shaped(8, slots), *(() if last else (pack, pack))),
            in_specs=specs + [vmem] * 4 + [smem],
            out_specs=(vmem,) * (3 if last else 5),
            scratch_shapes=[
                lhs_scratch,
                pltpu.VMEM(((planes + 2) * gy * gz, 3, slots, slots), F32),
            ],
            compiler_params=pltpu.CompilerParams(vmem_limit_bytes=26 * 2**20),
            cost_estimate=cost_f,
            name="force",
        )(*args, emb_lo, emb, emb_hi, motion, blocks)
        sums = [part] + [lax.ppermute(part, "space", ring("space", s)) for s in range(1, space)]
        if not last:
            packs = halo(*edges)
        if quench_step == 0:
            held = jnp.concatenate([start_pos, pushed], axis=0)
            for index in range(len(hops) - 1):
                options, pick = hop(index, held)
                held = options[0]
                for turn in range(1, len(options)):
                    held = jnp.where(pick == turn, options[turn], held)
            options, pick = hop(len(hops) - 1, held)

    quench_pos, quench_vel, place, drift = pl.pallas_call(
        functools.partial(finish_kernel, dims, len(options)),
        out_shape=(vec,) * 4,
        in_specs=[vmem] * 4 + [smem] * 2 + [vmem] * (len(options) + space),
        out_specs=(vmem,) * 4,
        compiler_params=pltpu.CompilerParams(vmem_limit_bytes=12 * 2**20),
        name="finish",
    )(coords[1], forces, pushed, thermal_noise[0, 0], counts, pick[None], *options, *sums)
    return quench_pos[None], quench_vel[None], place[None], drift[None]


def solution(mesh):
    vector = P("rep", None, "space", None, None, None)
    placed = (
        vector,
        vector,
        P("rep", None, None, "space", None, None, None),
        P("space", None, None),
        P(None, "space", None, None),
        P(),
    )
    return jax.shard_map(body, mesh=mesh, in_specs=placed, out_specs=(vector,) * 4, check_vma=False)
```

```python
import functools
import math

import jax
import jax.numpy as jnp
import numpy as np
from jax import lax
from jax.experimental import pallas as pl
from jax.experimental.pallas import tpu as pltpu
from jax.sharding import PartitionSpec as P


QUENCH = 2
STEP_SIZE = 0.1
ALPHA_MIX = 0.25
EPSILON = 1e-06
FRICTION = math.exp(-0.2)
KICK_SCALE = math.sqrt(1.0 - FRICTION * FRICTION)
HALF_OFFSETS = (
    [(1, p, q) for p in (-1, 0, 1) for q in (-1, 0, 1)]
    + [(0, 1, q) for q in (-1, 0, 1)]
    + [(0, 0, 1)]
)
OFFSETS = [(i, j, k) for i in (-1, 0, 1) for j in (-1, 0, 1) for k in (-1, 0, 1)]
FAR = 1.0e6
BF = jnp.bfloat16
F32 = jnp.float32
KDIM = 64
TILE = 32
ITEM = 12
GROUP = 4


def ring(axis, shift):
    count = lax.axis_size(axis)
    return [(i, (i + shift) % count) for i in range(count)]


def flag_of(offset):
    for index, entry in enumerate(HALF_OFFSETS):
        if entry == offset:
            return index, True
        if entry == tuple(-v for v in offset):
            return index, False
    return None


def split3(value):
    high = value.astype(BF).astype(F32)
    rest = value - high
    mid = rest.astype(BF).astype(F32)
    return high, mid, (rest - mid).astype(BF).astype(F32)


def wrap(index, size):
    index = jnp.where(index < 0, index + size, index)
    return jnp.where(index >= size, index - size, index)


def list_sizes(dims, slots):
    cells = math.prod(dims)
    most = cells * (-(-27 * (slots // TILE) // ITEM))
    head = 8
    return head, most + 2 * GROUP, head + (most + 2 * GROUP) * (ITEM + 1) + 2 * ITEM


def build_list(dims, slots, cnt, flags, flags_lo, list_ref):
    planes, gy, gz = dims
    ey, ez = gy + 2, gz + 2
    per = slots // TILE
    dummy = (planes + 2) * ey * ez * per
    head, items, _ = list_sizes(dims, slots)
    tiles = head + items
    bound = -(-27 * per // ITEM)

    def count_at(j, y, z):
        which, at = (0, 0) if j == 0 else ((2, 0) if j == planes + 1 else (1, j - 1))
        return cnt[which][at, y, z]

    def cell_list(p, y, z, item):
        at = item * ITEM
        for ox, oy, oz in OFFSETS:
            ext = ((p + 1 + ox) * ey + (y + 1 + oy)) * ez + (z + 1 + oz)
            jy, jz = wrap(y + oy, gy), (z + oz) % gz
            number = (count_at(p + 1 + ox, jy, jz) + (TILE - 1)) // TILE
            found = flag_of((ox, oy, oz))
            if found is not None:
                index, forward = found
                if forward:
                    flag = flags[index, p, y, z]
                elif p + ox < 0:
                    flag = flags_lo[index, 0, jy, jz]
                else:
                    flag = flags[index, p + ox, jy, jz]
                number = number * flag
            for t in range(per):
                list_ref[tiles + at + t] = ext * per + t
            at = at + number
        for t in range(ITEM):
            list_ref[tiles + at + t] = dummy
        for t in range(bound):
            list_ref[head + item + t] = (p * gy + y) * gz + z
        return (at + (ITEM - 1)) // ITEM

    item = 0
    for p in range(planes):

        def row(y, item):
            for z in range(gz):
                item = cell_list(p, y, z, item)
            return item

        item = lax.fori_loop(0, gy, row, item)
    list_ref[0] = (item + (GROUP - 1)) // GROUP * GROUP

    def rest(i, _):
        list_ref[head + item + i] = planes * gy * gz - 1
        for t in range(ITEM):
            list_ref[tiles + (item + i) * ITEM + t] = dummy
        return 0

    lax.fori_loop(0, 2 * GROUP - 1, rest, 0)


def build_partners(dims, pos, cnt, emb, lhs_ref, wide_refs, *accs):
    planes, gy, gz = dims
    ey, ez = gy + 2, gz + 2
    slots = lhs_ref.shape[1]
    full = (8, slots)
    rows = lax.broadcasted_iota(jnp.int32, full, 0)
    lane = lax.broadcasted_iota(jnp.int32, full, 1)
    blank = jnp.zeros((slots - KDIM, slots), F32)

    def store(ext, value):
        h, m, l = split3(value)
        tall = jnp.concatenate([h, h, h, m, m, m, l, l, blank], axis=0).T.astype(BF)
        lhs_ref[ext] = tall
        return tall

    if wide_refs is not None:
        row = lax.broadcasted_iota(jnp.int32, (2 * slots, 2 * slots), 0)
        col = lax.broadcasted_iota(jnp.int32, (2 * slots, 2 * slots), 1) // slots
        used = (row < 8) | ((row >= 24) & (row < 32)) | ((row >= 48) & (row < 56))
        side = jnp.zeros((slots, slots), BF)
        wide_x, wide_y, wide_z = wide_refs
        acc_xy, acc_z = accs[:gz], accs[gz:]
        for m, base in enumerate((0, 2)):
            pick = jnp.where(used & (row % 8 == col + base) & (col + base < 3), 1.0, 0.0)
            pltpu.matmul_push_rhs(pick.astype(BF), staging_register=0, mxu_index=m)
        for m in range(2):
            for index, acc in enumerate((acc_xy, acc_z)[m]):
                pltpu.matmul_acc_lhs(
                    acc,
                    jnp.zeros((slots, 2 * slots), BF),
                    load_staged_rhs=0 if index == 0 else None,
                )

    def one(j, which, at, y, z, by, bz):
        raw = [
            jnp.broadcast_to(pos[which][k, at, by, pl.ds(bz, 1), :], full) for k in range(3)
        ]
        xx = raw[0] + (j - 0.5 - (planes + 1) / 2)
        yy = raw[1] + (jnp.asarray(y).astype(F32) - 0.5 - (gy + 1) / 2)
        zz = raw[2] + (z - 0.5 - (gz + 1) / 2)
        norm = xx * xx + yy * yy + zz * zz
        norm = jnp.where(lane < cnt[which][at, by, bz], norm, norm + FAR)
        value = jnp.where(rows == 0, xx, jnp.where(rows == 1, yy, zz))
        value = jnp.where(rows == 3, norm, value)
        value = jnp.where(rows >= 4, 1.0, value)
        if emb is not None:
            e = jnp.broadcast_to(emb[which][at, by, pl.ds(bz, 1), :], full) * 0.25
            value = jnp.where(rows == 6, e, value)
        return store((j * ey + y) * ez + z, value)

    def put(spot):
        at_x, at_y, at_z = spot
        for z in range(gz):
            both = pltpu.matmul_pop(acc_xy[z])
            wide_x[at_x + z] = both[:, :slots]
            wide_y[at_y + z] = both[:, slots:]
        for z in range(ez):
            wide_z[at_z + z] = pltpu.matmul_pop(acc_z[z])[:, :slots]

    spot = (jnp.int32(0),) * 3
    for j in range(planes + 2):
        which, at = (0, 0) if j == 0 else ((2, 0) if j == planes + 1 else (1, j - 1))

        def line(y, spot):
            by = wrap(y - 1, gy)
            talls = [one(j, which, at, y, z, by, (z - 1) % gz) for z in range(ez)]
            if wide_refs is None:
                return spot
            put(spot)
            for z in range(ez):
                left = jnp.concatenate([talls[z], side], axis=1)
                if 1 <= z <= gz:
                    pltpu.matmul_acc_lhs(acc_xy[z - 1], left)
                pltpu.matmul_acc_lhs(acc_z[z], left)
            return ((j * gy + by) * gz, (j * ey + y) * gz, (j * gy + by) * ez)

        spot = lax.fori_loop(0, ey, line, spot)
    if wide_refs is not None:
        put(spot)
    store((planes + 2) * ey * ez, jnp.where(rows == 3, FAR, jnp.where(rows >= 4, 1.0, 0.0)))


def wide_table(dims, slots):
    planes, gy, gz = dims
    ey, ez = gy + 2, gz + 2
    per = slots // TILE
    table = np.zeros(((planes + 2) * ey * ez + 1) * per, np.int32)
    for j in range(planes + 2):
        for y in range(ey):
            for z in range(ez):
                by, bz = (y - 1) % gy, (z - 1) % gz
                where = ((j * gy + by) * gz + bz, (j * ey + y) * gz + bz, (j * gy + by) * ez + z)
                for t in range(per):
                    x0, y0, z0 = (w * per + t for w in where)
                    table[((j * ey + y) * ez + z) * per + t] = x0 | (y0 << 10) | (z0 << 20)
    return table


def build_center(dims, p, y, z, x3, count, e_row):
    planes, gy, gz = dims
    slots = x3[0].shape[-1]
    full = (8, slots)
    rows = lax.broadcasted_iota(jnp.int32, full, 0)
    lane = lax.broadcasted_iota(jnp.int32, full, 1)
    xx = jnp.broadcast_to(x3[0], full) + (p + 0.5 - (planes + 1) / 2)
    yy = jnp.broadcast_to(x3[1], full) + (y.astype(F32) + 0.5 - (gy + 1) / 2)
    zz = jnp.broadcast_to(x3[2], full) + (z.astype(F32) + 0.5 - (gz + 1) / 2)
    one = 1.0 - (xx * xx + yy * yy + zz * zz)
    one = jnp.where(lane < count, one, one - FAR)
    value = jnp.where(rows == 0, xx, jnp.where(rows == 1, yy, zz)) * 2.0
    value = jnp.where(rows == 4, one, value)
    if e_row is not None:
        value = jnp.where(rows == 5, jnp.broadcast_to(e_row, full) * 0.25, value)
    parts = split3(value)
    us, ws = [], []
    for block in range(8):
        part = parts[block % 3]
        keep = rows < 3
        if block < 3:
            keep = keep | (rows == 4)
        u = jnp.where(keep, part, 0.0)
        if block % 3 == 0:
            u = jnp.where(rows == 3, -1.0, u)
        us.append(u)
        if e_row is not None:
            w = u
            if block < 3:
                w = jnp.where(rows == 5, part, w)
            if block % 3 == 0:
                w = jnp.where(rows == 6, 1.0, w)
            ws.append(w)
    right = jnp.concatenate(us, axis=0).astype(BF)
    if e_row is None:
        return right
    return jnp.concatenate([right, jnp.concatenate(ws, axis=0).astype(BF)], axis=1)


def mix_factor(sum_refs):
    total = sum_refs[0][...]
    for ref in sum_refs[1:]:
        total = total + ref[...]
    force_sq = jnp.sum(total[0:1], axis=1, keepdims=True)
    vel_sq = jnp.sum(total[1:2], axis=1, keepdims=True)
    return jnp.sqrt(vel_sq / (force_sq + EPSILON))


def quench_update(dims, mix, x_ref, f_of, v_of, planes, x_out, v_out):
    gy, _ = dims[1:]
    for k in range(3):
        for p in range(planes):
            for y in range(gy):
                v = (1.0 - ALPHA_MIX) * v_of(k, p, y) + ALPHA_MIX * mix * f_of(k, p, y)
                if v_out is not None:
                    v_out[k, p, y] = v
                x_out[k, p, y] = x_ref[k, p, y] + STEP_SIZE * v


def density_kernel(dims, first, *refs):
    planes, gy, gz = dims
    if first:
        (p0, p1, p2, c0, c1, c2, fl, fl_lo, emb_ref, lo_ref, hi_ref, list_ref, lhs_ref, right_ref, res_ref) = refs
        build_list(dims, lhs_ref.shape[1], (c0, c1, c2), fl, fl_lo, list_ref)
    else:
        (q0, q1, q2, c0, c1, c2, list_ref, f_ref, v_ref, b0, b2) = refs[:11]
        sum_refs = refs[11:-10]
        (emb_ref, lo_ref, hi_ref, p0, p1, p2, v_out, lhs_ref, right_ref, res_ref) = refs[-10:]
        mix = mix_factor(sum_refs)
        quench_update(
            dims, mix, q1, lambda k, p, y: f_ref[k, p, y], lambda k, p, y: v_ref[k, p, y], planes, p1, v_out
        )
        for q, b, out in ((q0, b0, p0), (q2, b2, p2)):
            quench_update(
                dims, mix, q, lambda k, p, y, b=b: b[k, p, y], lambda k, p, y, b=b: b[k + 3, p, y], 1, out, None
            )
    slots = lhs_ref.shape[1]
    build_partners(dims, (p0, p1, p2), (c0, c1, c2), None, lhs_ref, None)
    build_rights(dims, p1, c1, None, right_ref)
    gap = jnp.zeros((slots - KDIM, slots), BF)
    side = jnp.zeros((slots, slots), BF)

    def right_of(cell):
        one = jnp.concatenate([right_ref[cell], gap], axis=0)
        return jnp.concatenate(
            [jnp.concatenate([one, side], axis=1), jnp.concatenate([side, one], axis=1)], axis=0
        )

    def left_of(tiles):
        return jnp.concatenate([load_tile(lhs_ref, t) for t in tiles], axis=1)

    def work(tiles, value, acc):
        for r in range(TILE // 8):
            for h in range(2):
                t = jnp.maximum(value[r * 8 : r * 8 + 8, h * slots : (h + 1) * slots], 0.0)
                acc[r] = acc[r] + t * t * t

    def emit(cell, acc):
        res_ref[cell] = (acc[0] + acc[1]) + (acc[2] + acc[3])

    run_items(dims, slots, list_ref, GROUP, 2, 4, right_of, left_of, work, emit)
    lane = lax.broadcasted_iota(jnp.int32, (1, slots), 1)
    for p in range(planes):

        def row(y, _):
            for z in range(gz):
                total = jnp.sum(res_ref[(p * gy + y) * gz + z], axis=0, keepdims=True)
                total = total - jnp.where(lane < c1[p, y, z], 1.0, 0.0)
                emb = -lax.rsqrt(1.0 + total / slots)
                emb_ref[p, y, z : z + 1, :] = emb
                if p == 0:
                    lo_ref[0, y, z : z + 1, :] = emb
                if p == planes - 1:
                    hi_ref[0, y, z : z + 1, :] = emb
            return 0

        lax.fori_loop(0, gy, row, 0)


def load_tile(ref, index):
    per = ref.shape[1] // TILE
    return ref[index // per, pl.ds(pl.multiple_of((index % per) * TILE, TILE), TILE), :]


def build_rights(dims, pos, cnt, emb, right_ref):
    planes, gy, gz = dims
    for p in range(planes):

        def row(y, _):
            for z in range(gz):
                x3 = [pos[k, p, y, z : z + 1, :] for k in range(3)]
                e_row = None if emb is None else emb[p, y, z : z + 1, :]
                right_ref[(p * gy + y) * gz + z] = build_center(
                    dims, p, y, jnp.int32(z), x3, cnt[p, y, z], e_row
                )
            return 0

        lax.fori_loop(0, gy, row, 0)


def run_items(dims, slots, list_ref, group, width, chains, right_of, left_of, work, emit):
    head, items, _ = list_sizes(dims, slots)
    tiles_at = head + items
    turns = ITEM // (2 * width)

    def inner(*flat):
        accs = [
            [[flat[(i * 2 + m) * turns + t] for t in range(turns)] for m in range(2)]
            for i in range(group)
        ]

        def tile_ids(item, m, t):
            return [list_ref[tiles_at + item * ITEM + (t * 2 + m) * width + w] for w in range(width)]

        def load_right(item):
            right = right_of(list_ref[head + item])
            for m in range(2):
                pltpu.matmul_push_rhs(right, staging_register=0, mxu_index=m)

        def send(item, i, m, t):
            pltpu.matmul_acc_lhs(
                accs[i][m][t],
                left_of(tile_ids(item, m, t)),
                load_staged_rhs=0 if t == 0 else None,
            )

        for i in range(group):
            load_right(i)
            for t in range(turns):
                for m in range(2):
                    send(i, i, m, t)

        def step(turn, carry):
            acc = list(carry)
            for i in range(group):
                item = turn * group + i
                cell = list_ref[head + item]
                same = cell == list_ref[head + jnp.maximum(item - 1, 0)]
                keep = same.astype(F32)
                acc = [value * keep for value in acc]
                load_right(item + group)
                for t in range(turns):
                    for m in range(2):
                        value = pltpu.matmul_pop(accs[i][m][t])
                        send(item + group, i, m, t)
                        work(tile_ids(item, m, t), value, acc)
                emit(cell, acc)
            return tuple(acc)

        zero = jnp.zeros((8, slots), F32)
        lax.fori_loop(0, list_ref[0] // group, step, (zero,) * chains)
        for i in range(group):
            for t in range(turns):
                for m in range(2):
                    pltpu.matmul_pop(accs[i][m][t])

    pl.run_scoped(
        inner,
        *[
            pltpu.ACC(m)((TILE, 2 * slots), F32)
            for _ in range(group)
            for m in range(2)
            for _ in range(turns)
        ],
    )


def force_kernel(dims, *refs):
    (p0, p1, p2, c0, c1, c2, e0, e1, e2, vel, list_ref, table_ref) = refs[:12]
    (f_ref, v_ref, s_ref) = refs[12:15]
    edges = refs[15:-6]
    (lhs_ref, right_ref, res_ref, *wide_refs) = refs[-6:]
    planes, gy, gz = dims
    slots = lhs_ref.shape[1]
    pl.run_scoped(
        functools.partial(build_partners, dims, (p0, p1, p2), (c0, c1, c2), (e0, e1, e2), lhs_ref, wide_refs),
        *[pltpu.ACC(m)((slots, 2 * slots), F32) for m in range(2) for _ in range(gz + 2 * m)],
    )
    build_rights(dims, p1, c1, e1, right_ref)
    gap = jnp.zeros((2 * slots - KDIM, 2 * slots), BF)
    side = jnp.zeros((TILE, slots), BF)

    def right_of(cell):
        return jnp.concatenate([right_ref[cell], gap], axis=0)

    def left_of(tiles):
        return jnp.concatenate([load_tile(lhs_ref, tiles[0]), side], axis=1)

    def work(tiles, value, acc):
        where = table_ref[tiles[0]]
        spots = (where & 1023, (where >> 10) & 1023, where >> 20)
        wides = [load_tile(ref, spot) for ref, spot in zip(wide_refs, spots)]
        for r in range(TILE // 8):
            here = slice(r * 8, r * 8 + 8)
            t = jnp.maximum(value[here, :slots], 0.0)
            g = t * t * value[here, slots:]
            half = (r % 2) * 4
            acc[half] = acc[half] + g
            for k in range(3):
                acc[half + 1 + k] = acc[half + 1 + k] + g * wides[k][here]

    def emit(cell, acc):
        for k in range(4):
            res_ref[cell, k] = acc[k] + acc[k + 4]

    run_items(dims, slots, list_ref, 2, 1, 8, right_of, left_of, work, emit)
    lane = lax.broadcasted_iota(jnp.int32, (1, slots), 1)
    sums = (jnp.zeros((1, slots), F32), jnp.zeros((1, slots), F32))
    for p in range(planes):

        def row(y, sums):
            ff, vv = sums
            for z in range(gz):
                cell = (p * gy + y) * gz + z
                one = slice(z, z + 1)
                center = (
                    p + 0.5 - (planes + 1) / 2,
                    y.astype(F32) + 0.5 - (gy + 1) / 2,
                    z + 0.5 - (gz + 1) / 2,
                )
                total = jnp.sum(res_ref[cell, 0], axis=0, keepdims=True)
                for k in range(3):
                    x = p1[k, p, y, one, :] + center[k]
                    f = (24.0 / slots) * (x * total - jnp.sum(res_ref[cell, k + 1], axis=0, keepdims=True))
                    f_ref[k, p, y, one, :] = f
                    v = jnp.where(lane < c1[p, y, z], vel[k, p, y, one, :], 0.0) + STEP_SIZE * f
                    v_ref[k, p, y, one, :] = v
                    if edges and p == 0:
                        edges[0][k, 0, y, one, :] = f
                        edges[0][k + 3, 0, y, one, :] = v
                    if edges and p == planes - 1:
                        edges[1][k, 0, y, one, :] = f
                        edges[1][k + 3, 0, y, one, :] = v
                    ff = ff + f * f
                    vv = vv + v * v
            return ff, vv

        sums = lax.fori_loop(0, gy, row, sums)
    s_ref[...] = jnp.concatenate([sums[0], sums[1], jnp.zeros((6, slots), F32)], axis=0)


def finish_kernel(dims, radix, *refs):
    (x_ref, f_ref, v_ref, noise, cnt, pick) = refs[:6]
    options = refs[6 : 6 + radix]
    sum_refs = refs[6 + radix : -4]
    (xq, vq, xd, vd) = refs[-4:]
    planes, gy, gz = dims
    slots = x_ref.shape[-1]
    mix = mix_factor(sum_refs)
    quench_update(
        dims, mix, x_ref, lambda k, p, y: f_ref[k, p, y], lambda k, p, y: v_ref[k, p, y], planes, xq, vq
    )
    lane = lax.broadcasted_iota(jnp.int32, (gz, slots), 1)
    line = lax.broadcasted_iota(jnp.int32, (gz, slots), 0)
    take = pick[0]
    for p in range(planes):
        for y in range(gy):
            limit = jnp.zeros((gz, slots), jnp.int32)
            for z in range(gz):
                limit = jnp.where(line == z, cnt[p, y, z], limit)
            occupied = (lane < limit).astype(F32)
            for k in range(3):
                place, push = options[0][k, p, y], options[0][k + 3, p, y]
                for index in range(1, radix):
                    place = jnp.where(take == index, options[index][k, p, y], place)
                    push = jnp.where(take == index, options[index][k + 3, p, y], push)
                v = FRICTION * push + KICK_SCALE * occupied * noise[k, p, y]
                vd[k, p, y] = v
                xd[k, p, y] = place + STEP_SIZE * v


def exit_hops(count):
    hops, stride = [], 1
    while stride < count:
        left = count // stride
        radix = next(r for r in (4, 2, 3, 5, 7, left) if left % r == 0)
        hops.append((stride, radix))
        stride *= radix
    return hops


def body(positions, velocities, thermal_noise, counts, pair_flags, exit_replica):
    start_pos = positions[0]
    start_vel = velocities[0]
    planes, gy, gz, slots = start_pos.shape[1:]
    dims = (planes, gy, gz)
    up, down = ring("space", 1), ring("space", -1)
    space = lax.axis_size("space")
    vmem = pl.BlockSpec(memory_space=pltpu.VMEM)
    smem = pl.BlockSpec(memory_space=pltpu.SMEM)
    ext = (planes + 2) * (gy + 2) * (gz + 2) + 1
    cells = planes * gy * gz
    entries = list_sizes(dims, slots)[2]
    table = jnp.asarray(wide_table(dims, slots))
    pairs = planes * gy * gz * 27 * slots * slots

    def shaped(*shape):
        return jax.ShapeDtypeStruct(shape, F32)

    def planes_of(block, dim):
        return lax.slice_in_dim(block, 0, 1, axis=dim), lax.slice_in_dim(block, planes - 1, planes, axis=dim)

    def halo(first, last):
        return lax.ppermute(last, "space", up), lax.ppermute(first, "space", down)

    flags_lo = lax.ppermute(lax.slice_in_dim(pair_flags, planes - 1, planes, axis=1), "space", up)
    count_lo, count_hi = halo(*planes_of(counts, 0))
    pos_lo, pos_hi = halo(*planes_of(start_pos, 1))
    lhs_scratch = pltpu.VMEM((ext, slots, slots), BF)
    scratch_d = [lhs_scratch, pltpu.VMEM((cells, KDIM, slots), BF), pltpu.VMEM((cells, 8, slots), F32)]
    scratch_f = [
        lhs_scratch,
        pltpu.VMEM((cells, KDIM, 2 * slots), BF),
        pltpu.VMEM((cells, 4, 8, slots), F32),
        pltpu.VMEM(((planes + 2) * gy * gz, slots, slots), F32),
        pltpu.VMEM(((planes + 2) * (gy + 2) * gz, slots, slots), F32),
        pltpu.VMEM(((planes + 2) * gy * (gz + 2), slots, slots), F32),
    ]
    emb_shape = [shaped(planes, gy, gz, slots), shaped(1, gy, gz, slots), shaped(1, gy, gz, slots)]
    vec, edge = shaped(3, planes, gy, gz, slots), shaped(3, 1, gy, gz, slots)
    pack = shaped(6, 1, gy, gz, slots)
    number = [smem] * 3
    cost_d = pl.CostEstimate(flops=pairs * 10, bytes_accessed=2**20, transcendentals=0)
    cost_f = pl.CostEstimate(flops=pairs * 25, bytes_accessed=2**20, transcendentals=0)

    held, hops = None, exit_hops(lax.axis_size("rep"))
    me, chosen = lax.axis_index("rep"), exit_replica[0]

    def hop(index, held):
        stride, radix = hops[index]
        digit, root = (me // stride) % radix, (chosen // stride) % radix
        options = [held]
        for turn in range(1, radix):
            pairs = []
            for i in range(lax.axis_size("rep")):
                at = (i // stride) % radix
                pairs.append((i, i + (((at + turn) % radix) - at) * stride))
            options.append(lax.ppermute(held, "rep", pairs))
        return options, (digit - root) % radix

    motion = start_vel
    coords = (pos_lo, start_pos, pos_hi)
    for quench_step in range(QUENCH):
        args = [*coords, count_lo, counts, count_hi]
        specs = [vmem] * 3 + number
        if quench_step == 0:
            emb, emb_first, emb_last, blocks = pl.pallas_call(
                functools.partial(density_kernel, dims, True),
                out_shape=(*emb_shape, jax.ShapeDtypeStruct((entries,), jnp.int32)),
                in_specs=specs + [smem, smem],
                out_specs=(vmem, vmem, vmem, smem),
                scratch_shapes=scratch_d,
                compiler_params=pltpu.CompilerParams(vmem_limit_bytes=12 * 2**20),
                cost_estimate=cost_d,
                name="density_first",
            )(*args, pair_flags, flags_lo)
        else:
            emb, emb_first, emb_last, *coords, motion = pl.pallas_call(
                functools.partial(density_kernel, dims, False),
                out_shape=(*emb_shape, edge, vec, edge, vec),
                in_specs=specs + [smem] + [vmem] * (4 + space),
                out_specs=(vmem,) * 7,
                scratch_shapes=scratch_d,
                compiler_params=pltpu.CompilerParams(vmem_limit_bytes=12 * 2**20),
                cost_estimate=cost_d,
                name="density_next",
            )(*args, blocks, forces, pushed, *packs, *sums)
            args = [*coords, count_lo, counts, count_hi]
        emb_lo, emb_hi = halo(emb_first, emb_last)
        last = quench_step == QUENCH - 1
        forces, pushed, part, *edges = pl.pallas_call(
            functools.partial(force_kernel, dims),
            out_shape=(vec, vec, shaped(8, slots), *(() if last else (pack, pack))),
            in_specs=specs + [vmem] * 4 + [smem] * 2,
            out_specs=(vmem,) * (3 if last else 5),
            scratch_shapes=scratch_f,
            compiler_params=pltpu.CompilerParams(vmem_limit_bytes=34 * 2**20),
            cost_estimate=cost_f,
            name="force",
        )(*args, emb_lo, emb, emb_hi, motion, blocks, table)
        sums = [part] + [lax.ppermute(part, "space", ring("space", s)) for s in range(1, space)]
        if not last:
            packs = halo(*edges)
        if quench_step == 0:
            held = jnp.concatenate([start_pos, pushed], axis=0)
            for index in range(len(hops) - 1):
                options, pick = hop(index, held)
                held = options[0]
                for turn in range(1, len(options)):
                    held = jnp.where(pick == turn, options[turn], held)
            options, pick = hop(len(hops) - 1, held)

    quench_pos, quench_vel, place, drift = pl.pallas_call(
        functools.partial(finish_kernel, dims, len(options)),
        out_shape=(vec,) * 4,
        in_specs=[vmem] * 4 + [smem] * 2 + [vmem] * (len(options) + space),
        out_specs=(vmem,) * 4,
        compiler_params=pltpu.CompilerParams(vmem_limit_bytes=12 * 2**20),
        name="finish",
    )(coords[1], forces, pushed, thermal_noise[0, 0], counts, pick[None], *options, *sums)
    return quench_pos[None], quench_vel[None], place[None], drift[None]


def solution(mesh):
    vector = P("rep", None, "space", None, None, None)
    placed = (
        vector,
        vector,
        P("rep", None, None, "space", None, None, None),
        P("space", None, None),
        P(None, "space", None, None),
        P(),
    )
    return jax.shard_map(body, mesh=mesh, in_specs=placed, out_specs=(vector,) * 4, check_vma=False)
```

```python
import functools
import math

import jax
import jax.numpy as jnp
from jax import lax
from jax.experimental import pallas as pl
from jax.experimental.pallas import tpu as pltpu
from jax.sharding import PartitionSpec as P


QUENCH = 2
STEP_SIZE = 0.1
ALPHA_MIX = 0.25
EPSILON = 1e-06
FRICTION = math.exp(-0.2)
KICK_SCALE = math.sqrt(1.0 - FRICTION * FRICTION)
HALF_OFFSETS = (
    [(1, p, q) for p in (-1, 0, 1) for q in (-1, 0, 1)]
    + [(0, 1, q) for q in (-1, 0, 1)]
    + [(0, 0, 1)]
)
OFFSETS = [(i, j, k) for i in (-1, 0, 1) for j in (-1, 0, 1) for k in (-1, 0, 1)]
FAR = 1.0e6
BF = jnp.bfloat16
F32 = jnp.float32
KDIM = 64
ITEM = 3
GROUP = 4


def ring(axis, shift):
    count = lax.axis_size(axis)
    return [(i, (i + shift) % count) for i in range(count)]


def flag_of(offset):
    for index, entry in enumerate(HALF_OFFSETS):
        if entry == offset:
            return index, True
        if entry == tuple(-v for v in offset):
            return index, False
    return None


def split3(value):
    high = value.astype(BF).astype(F32)
    rest = value - high
    mid = rest.astype(BF).astype(F32)
    return high, mid, (rest - mid).astype(BF).astype(F32)


def wrap(index, size):
    index = jnp.where(index < 0, index + size, index)
    return jnp.where(index >= size, index - size, index)


def list_sizes(dims):
    most = math.prod(dims) * -(-27 // ITEM)
    head = 8
    return head, most + 2 * GROUP, head + (most + 2 * GROUP) * (ITEM + 1) + 2 * ITEM


def build_list(dims, flags, flags_lo, list_ref):
    planes, gy, gz = dims
    ey, ez = gy + 2, gz + 2
    dummy = (planes + 2) * ey * ez
    head, items, _ = list_sizes(dims)
    entries = head + items
    bound = -(-27 // ITEM)

    def cell_list(p, y, z, item):
        at = item * ITEM
        for ox, oy, oz in OFFSETS:
            list_ref[entries + at] = ((p + 1 + ox) * ey + (y + 1 + oy)) * ez + (z + 1 + oz)
            found = flag_of((ox, oy, oz))
            if found is None:
                at = at + 1
                continue
            index, forward = found
            jy, jz = wrap(y + oy, gy), (z + oz) % gz
            if forward:
                flag = flags[index, p, y, z]
            elif p + ox < 0:
                flag = flags_lo[index, 0, jy, jz]
            else:
                flag = flags[index, p + ox, jy, jz]
            at = at + flag
        for t in range(ITEM):
            list_ref[entries + at + t] = dummy
        for t in range(bound):
            list_ref[head + item + t] = (p * gy + y) * gz + z
        return (at + (ITEM - 1)) // ITEM

    item = 0
    for p in range(planes):

        def row(y, item):
            for z in range(gz):
                item = cell_list(p, y, z, item)
            return item

        item = lax.fori_loop(0, gy, row, item)
    list_ref[0] = (item + (GROUP - 1)) // GROUP * GROUP

    def rest(i, _):
        list_ref[head + item + i] = planes * gy * gz - 1
        for t in range(ITEM):
            list_ref[entries + (item + i) * ITEM + t] = dummy
        return 0

    lax.fori_loop(0, 2 * GROUP - 1, rest, 0)


def build_partners(dims, pos, cnt, emb, lhs_ref, wide_ref, *accs):
    planes, gy, gz = dims
    ey, ez = gy + 2, gz + 2
    slots = lhs_ref.shape[1]
    full = (8, slots)
    rows = lax.broadcasted_iota(jnp.int32, full, 0)
    lane = lax.broadcasted_iota(jnp.int32, full, 1)
    blank = jnp.zeros((slots - KDIM, slots), F32)

    def store(ext, value):
        h, m, l = split3(value)
        tall = jnp.concatenate([h, h, h, m, m, m, l, l, blank], axis=0).T.astype(BF)
        lhs_ref[ext] = tall
        return tall

    if wide_ref is not None:
        row = lax.broadcasted_iota(jnp.int32, (2 * slots, 2 * slots), 0)
        col = lax.broadcasted_iota(jnp.int32, (2 * slots, 2 * slots), 1) // slots
        line_row = row % slots
        used = (line_row < 8) | ((line_row >= 24) & (line_row < 32)) | ((line_row >= 48) & (line_row < 56))
        side = jnp.zeros((slots, slots), BF)
        half = slots // 2
        acc_xy, acc_z = accs[:gz], accs[gz:]
        for m in range(2):
            if m == 0:
                chosen = used & (row < slots) & (line_row % 8 == col)
            else:
                chosen = used & (row // slots == col) & (line_row % 8 == 2)
            pick = jnp.where(chosen, 1.0, 0.0)
            pltpu.matmul_push_rhs(pick.astype(BF), staging_register=0, mxu_index=m)
        for m in range(2):
            for index, acc in enumerate((acc_xy, acc_z)[m]):
                pltpu.matmul_acc_lhs(
                    acc,
                    jnp.zeros((slots if m == 0 else half, 2 * slots), BF),
                    load_staged_rhs=0 if index == 0 else None,
                )

    def one(j, which, at, y, z, by, bz):
        raw = [
            jnp.broadcast_to(pos[which][k, at, by, pl.ds(bz, 1), :], full) for k in range(3)
        ]
        xx = raw[0] + (j - 0.5 - (planes + 1) / 2)
        yy = raw[1] + (jnp.asarray(y).astype(F32) - 0.5 - (gy + 1) / 2)
        zz = raw[2] + (z - 0.5 - (gz + 1) / 2)
        norm = xx * xx + yy * yy + zz * zz
        norm = jnp.where(lane < cnt[which][at, by, bz], norm, norm + FAR)
        value = jnp.where(rows == 0, xx, jnp.where(rows == 1, yy, zz))
        value = jnp.where(rows == 3, norm, value)
        value = jnp.where(rows >= 4, 1.0, value)
        if emb is not None:
            e = jnp.broadcast_to(emb[which][at, by, pl.ds(bz, 1), :], full) * 0.25
            value = jnp.where(rows == 6, e, value)
        return store((j * ey + y) * ez + z, value)

    def put(spot):
        for z in range(1, gz + 1):
            both = pltpu.matmul_pop(acc_xy[z - 1])
            for at in [z] + [0] * (z == gz) + [gz + 1] * (z == 1):
                wide_ref[spot + at, 0] = both[:, :slots]
                wide_ref[spot + at, 1] = both[:, slots:]
        for z in range(ez):
            both = pltpu.matmul_pop(acc_z[z])
            wide_ref[spot + z, 2, :half, :] = both[:, :slots]
            wide_ref[spot + z, 2, half:, :] = both[:, slots:]

    spot = jnp.int32(0)
    for j in range(planes + 2):
        which, at = (0, 0) if j == 0 else ((2, 0) if j == planes + 1 else (1, j - 1))

        def line(y, spot):
            by = wrap(y - 1, gy)
            talls = [one(j, which, at, y, z, by, (z - 1) % gz) for z in range(ez)]
            if wide_ref is None:
                return spot
            put(spot)
            for z in range(ez):
                if 1 <= z <= gz:
                    pltpu.matmul_acc_lhs(acc_xy[z - 1], jnp.concatenate([talls[z], side], axis=1))
                pltpu.matmul_acc_lhs(
                    acc_z[z], jnp.concatenate([talls[z][:half], talls[z][half:]], axis=1)
                )
            return (j * ey + y) * ez

        spot = lax.fori_loop(0, ey, line, spot)
    if wide_ref is not None:
        put(spot)
        for k in range(3):
            wide_ref[(planes + 2) * ey * ez, k] = jnp.zeros((slots, slots), F32)
    store((planes + 2) * ey * ez, jnp.where(rows == 3, FAR, jnp.where(rows >= 4, 1.0, 0.0)))


def build_center(dims, p, y, z, x3, count, e_row):
    planes, gy, gz = dims
    slots = x3[0].shape[-1]
    full = (8, slots)
    rows = lax.broadcasted_iota(jnp.int32, full, 0)
    lane = lax.broadcasted_iota(jnp.int32, full, 1)
    xx = jnp.broadcast_to(x3[0], full) + (p + 0.5 - (planes + 1) / 2)
    yy = jnp.broadcast_to(x3[1], full) + (y.astype(F32) + 0.5 - (gy + 1) / 2)
    zz = jnp.broadcast_to(x3[2], full) + (z.astype(F32) + 0.5 - (gz + 1) / 2)
    one = 1.0 - (xx * xx + yy * yy + zz * zz)
    one = jnp.where(lane < count, one, one - FAR)
    value = jnp.where(rows == 0, xx, jnp.where(rows == 1, yy, zz)) * 2.0
    value = jnp.where(rows == 4, one, value)
    if e_row is not None:
        value = jnp.where(rows == 5, jnp.broadcast_to(e_row, full) * 0.25, value)
    parts = split3(value)
    us, ws = [], []
    for block in range(8):
        part = parts[block % 3]
        keep = rows < 3
        if block < 3:
            keep = keep | (rows == 4)
        u = jnp.where(keep, part, 0.0)
        if block % 3 == 0:
            u = jnp.where(rows == 3, -1.0, u)
        us.append(u)
        if e_row is not None:
            w = u
            if block < 3:
                w = jnp.where(rows == 5, part, w)
            if block % 3 == 0:
                w = jnp.where(rows == 6, 1.0, w)
            ws.append(w)
    right = jnp.concatenate(us, axis=0).astype(BF)
    if e_row is None:
        return right
    return jnp.concatenate([right, jnp.concatenate(ws, axis=0).astype(BF)], axis=1)


def mix_factor(sum_refs):
    total = sum_refs[0][...]
    for ref in sum_refs[1:]:
        total = total + ref[...]
    force_sq = jnp.sum(total[0:1], axis=1, keepdims=True)
    vel_sq = jnp.sum(total[1:2], axis=1, keepdims=True)
    return jnp.sqrt(vel_sq / (force_sq + EPSILON))


def quench_update(dims, mix, x_ref, f_of, v_of, planes, x_out, v_out):
    gy, _ = dims[1:]
    for k in range(3):
        for p in range(planes):
            for y in range(gy):
                v = (1.0 - ALPHA_MIX) * v_of(k, p, y) + ALPHA_MIX * mix * f_of(k, p, y)
                if v_out is not None:
                    v_out[k, p, y] = v
                x_out[k, p, y] = x_ref[k, p, y] + STEP_SIZE * v


def density_kernel(dims, first, *refs):
    planes, gy, gz = dims
    if first:
        (p0, p1, p2, c0, c1, c2, fl, fl_lo, emb_ref, lo_ref, hi_ref, list_ref, lhs_ref, right_ref, res_ref) = refs
        build_list(dims, fl, fl_lo, list_ref)
    else:
        (q0, q1, q2, c0, c1, c2, list_ref, f_ref, v_ref, b0, b2) = refs[:11]
        sum_refs = refs[11:-10]
        (emb_ref, lo_ref, hi_ref, p0, p1, p2, v_out, lhs_ref, right_ref, res_ref) = refs[-10:]
        mix = mix_factor(sum_refs)
        quench_update(
            dims, mix, q1, lambda k, p, y: f_ref[k, p, y], lambda k, p, y: v_ref[k, p, y], planes, p1, v_out
        )
        for q, b, out in ((q0, b0, p0), (q2, b2, p2)):
            quench_update(
                dims, mix, q, lambda k, p, y, b=b: b[k, p, y], lambda k, p, y, b=b: b[k + 3, p, y], 1, out, None
            )
    slots = lhs_ref.shape[1]
    build_partners(dims, (p0, p1, p2), (c0, c1, c2), None, lhs_ref, None)
    build_rights(dims, p1, c1, None, right_ref)
    gap = jnp.zeros((slots - KDIM, slots), BF)
    side = jnp.zeros((slots, slots), BF)

    def right_of(cell):
        one = jnp.concatenate([right_ref[cell], gap], axis=0)
        return jnp.concatenate(
            [jnp.concatenate([one, side], axis=1), jnp.concatenate([side, one], axis=1)], axis=0
        )

    quarter = slots // 4

    def left_of(entry, m):
        start = m * 2 * quarter
        return jnp.concatenate(
            [lhs_ref[entry, start + h * quarter : start + (h + 1) * quarter, :] for h in range(2)], axis=1
        )

    def work(entry, m, value, acc):
        for r in range(quarter // 8):
            for h in range(2):
                t = jnp.maximum(value[r * 8 : r * 8 + 8, h * slots : (h + 1) * slots], 0.0)
                acc[r % 4] = acc[r % 4] + t * t * t

    def emit(cell, acc):
        res_ref[cell] = (acc[0] + acc[1]) + (acc[2] + acc[3])

    run_items(dims, slots, list_ref, GROUP, quarter, 4, right_of, left_of, work, emit)
    lane = lax.broadcasted_iota(jnp.int32, (1, slots), 1)
    for p in range(planes):

        def row(y, _):
            for z in range(gz):
                total = jnp.sum(res_ref[(p * gy + y) * gz + z], axis=0, keepdims=True)
                total = total - jnp.where(lane < c1[p, y, z], 1.0, 0.0)
                emb = -lax.rsqrt(1.0 + total / slots)
                emb_ref[p, y, z : z + 1, :] = emb
                if p == 0:
                    lo_ref[0, y, z : z + 1, :] = emb
                if p == planes - 1:
                    hi_ref[0, y, z : z + 1, :] = emb
            return 0

        lax.fori_loop(0, gy, row, 0)


def build_rights(dims, pos, cnt, emb, right_ref):
    planes, gy, gz = dims
    for p in range(planes):

        def row(y, _):
            for z in range(gz):
                x3 = [pos[k, p, y, z : z + 1, :] for k in range(3)]
                e_row = None if emb is None else emb[p, y, z : z + 1, :]
                right_ref[(p * gy + y) * gz + z] = build_center(
                    dims, p, y, jnp.int32(z), x3, cnt[p, y, z], e_row
                )
            return 0

        lax.fori_loop(0, gy, row, 0)


def run_items(dims, slots, list_ref, group, height, chains, right_of, left_of, work, emit):
    head, items, _ = list_sizes(dims)
    entries = head + items
    turns = ITEM

    def inner(*flat):
        accs = [
            [[flat[(i * 2 + m) * turns + t] for t in range(turns)] for m in range(2)]
            for i in range(group)
        ]

        def entry_of(item, t):
            return list_ref[entries + item * ITEM + t]

        def load_right(item):
            right = right_of(list_ref[head + item])
            for m in range(2):
                pltpu.matmul_push_rhs(right, staging_register=0, mxu_index=m)

        def send(item, i, m, t):
            pltpu.matmul_acc_lhs(
                accs[i][m][t],
                left_of(entry_of(item, t), m),
                load_staged_rhs=0 if t == 0 else None,
            )

        for i in range(group):
            load_right(i)
            for t in range(turns):
                for m in range(2):
                    send(i, i, m, t)

        def step(turn, carry):
            acc = list(carry)
            for i in range(group):
                item = turn * group + i
                cell = list_ref[head + item]
                same = cell == list_ref[head + jnp.maximum(item - 1, 0)]
                keep = same.astype(F32)
                acc = [value * keep for value in acc]
                load_right(item + group)
                for t in range(turns):
                    for m in range(2):
                        value = pltpu.matmul_pop(accs[i][m][t])
                        send(item + group, i, m, t)
                        work(entry_of(item, t), m, value, acc)
                emit(cell, acc)
            return tuple(acc)

        zero = jnp.zeros((8, slots), F32)
        lax.fori_loop(0, list_ref[0] // group, step, (zero,) * chains)
        for i in range(group):
            for t in range(turns):
                for m in range(2):
                    pltpu.matmul_pop(accs[i][m][t])

    pl.run_scoped(
        inner,
        *[
            pltpu.ACC(m)((height, 2 * slots), F32)
            for _ in range(group)
            for m in range(2)
            for _ in range(turns)
        ],
    )


def force_kernel(dims, *refs):
    (p0, p1, p2, c0, c1, c2, e0, e1, e2, vel, list_ref) = refs[:11]
    (f_ref, v_ref, s_ref) = refs[11:14]
    edges = refs[14:-4]
    (lhs_ref, right_ref, res_ref, wide_ref) = refs[-4:]
    planes, gy, gz = dims
    slots = lhs_ref.shape[1]
    pl.run_scoped(
        functools.partial(build_partners, dims, (p0, p1, p2), (c0, c1, c2), (e0, e1, e2), lhs_ref, wide_ref),
        *[pltpu.ACC(0)((slots, 2 * slots), F32) for _ in range(gz)],
        *[pltpu.ACC(1)((slots // 2, 2 * slots), F32) for _ in range(gz + 2)],
    )
    build_rights(dims, p1, c1, e1, right_ref)
    gap = jnp.zeros((2 * slots - KDIM, 2 * slots), BF)
    half = slots // 2
    side = jnp.zeros((half, slots), BF)

    def right_of(cell):
        return jnp.concatenate([right_ref[cell], gap], axis=0)

    def left_of(entry, m):
        return jnp.concatenate([lhs_ref[entry, m * half : (m + 1) * half, :], side], axis=1)

    def work(entry, m, value, acc):
        for r in range(half // 8):
            here = slice(r * 8, r * 8 + 8)
            t = jnp.maximum(value[here, :slots], 0.0)
            g = t * t * value[here, slots:]
            at = (r % 2) * 4
            acc[at] = acc[at] + g
            for k in range(3):
                acc[at + 1 + k] = acc[at + 1 + k] + g * wide_ref[entry, k, m * half + r * 8 : m * half + r * 8 + 8, :]

    def emit(cell, acc):
        for k in range(4):
            res_ref[cell, k] = acc[k] + acc[k + 4]

    run_items(dims, slots, list_ref, 2, half, 8, right_of, left_of, work, emit)
    lane = lax.broadcasted_iota(jnp.int32, (1, slots), 1)
    sums = (jnp.zeros((1, slots), F32), jnp.zeros((1, slots), F32))
    for p in range(planes):

        def row(y, sums):
            ff, vv = sums
            for z in range(gz):
                cell = (p * gy + y) * gz + z
                one = slice(z, z + 1)
                center = (
                    p + 0.5 - (planes + 1) / 2,
                    y.astype(F32) + 0.5 - (gy + 1) / 2,
                    z + 0.5 - (gz + 1) / 2,
                )
                total = jnp.sum(res_ref[cell, 0], axis=0, keepdims=True)
                for k in range(3):
                    x = p1[k, p, y, one, :] + center[k]
                    f = (24.0 / slots) * (x * total - jnp.sum(res_ref[cell, k + 1], axis=0, keepdims=True))
                    f_ref[k, p, y, one, :] = f
                    v = jnp.where(lane < c1[p, y, z], vel[k, p, y, one, :], 0.0) + STEP_SIZE * f
                    v_ref[k, p, y, one, :] = v
                    if edges and p == 0:
                        edges[0][k, 0, y, one, :] = f
                        edges[0][k + 3, 0, y, one, :] = v
                    if edges and p == planes - 1:
                        edges[1][k, 0, y, one, :] = f
                        edges[1][k + 3, 0, y, one, :] = v
                    ff = ff + f * f
                    vv = vv + v * v
            return ff, vv

        sums = lax.fori_loop(0, gy, row, sums)
    s_ref[...] = jnp.concatenate([sums[0], sums[1], jnp.zeros((6, slots), F32)], axis=0)


def finish_kernel(dims, radix, *refs):
    (x_ref, f_ref, v_ref, noise, cnt, pick) = refs[:6]
    options = refs[6 : 6 + radix]
    sum_refs = refs[6 + radix : -4]
    (xq, vq, xd, vd) = refs[-4:]
    planes, gy, gz = dims
    slots = x_ref.shape[-1]
    mix = mix_factor(sum_refs)
    quench_update(
        dims, mix, x_ref, lambda k, p, y: f_ref[k, p, y], lambda k, p, y: v_ref[k, p, y], planes, xq, vq
    )
    lane = lax.broadcasted_iota(jnp.int32, (gz, slots), 1)
    line = lax.broadcasted_iota(jnp.int32, (gz, slots), 0)
    take = pick[0]
    for p in range(planes):
        for y in range(gy):
            limit = jnp.zeros((gz, slots), jnp.int32)
            for z in range(gz):
                limit = jnp.where(line == z, cnt[p, y, z], limit)
            occupied = (lane < limit).astype(F32)
            for k in range(3):
                place, push = options[0][k, p, y], options[0][k + 3, p, y]
                for index in range(1, radix):
                    place = jnp.where(take == index, options[index][k, p, y], place)
                    push = jnp.where(take == index, options[index][k + 3, p, y], push)
                v = FRICTION * push + KICK_SCALE * occupied * noise[k, p, y]
                vd[k, p, y] = v
                xd[k, p, y] = place + STEP_SIZE * v


def exit_hops(count):
    hops, stride = [], 1
    while stride < count:
        left = count // stride
        radix = next(r for r in (4, 2, 3, 5, 7, left) if left % r == 0)
        hops.append((stride, radix))
        stride *= radix
    return hops


def body(positions, velocities, thermal_noise, counts, pair_flags, exit_replica):
    start_pos = positions[0]
    start_vel = velocities[0]
    planes, gy, gz, slots = start_pos.shape[1:]
    dims = (planes, gy, gz)
    up, down = ring("space", 1), ring("space", -1)
    space = lax.axis_size("space")
    vmem = pl.BlockSpec(memory_space=pltpu.VMEM)
    smem = pl.BlockSpec(memory_space=pltpu.SMEM)
    ext = (planes + 2) * (gy + 2) * (gz + 2) + 1
    cells = planes * gy * gz
    entries = list_sizes(dims)[2]
    pairs = planes * gy * gz * 27 * slots * slots

    def shaped(*shape):
        return jax.ShapeDtypeStruct(shape, F32)

    def planes_of(block, dim):
        return lax.slice_in_dim(block, 0, 1, axis=dim), lax.slice_in_dim(block, planes - 1, planes, axis=dim)

    def halo(first, last):
        return lax.ppermute(last, "space", up), lax.ppermute(first, "space", down)

    flags_lo = lax.ppermute(lax.slice_in_dim(pair_flags, planes - 1, planes, axis=1), "space", up)
    count_lo, count_hi = halo(*planes_of(counts, 0))
    pos_lo, pos_hi = halo(*planes_of(start_pos, 1))
    lhs_scratch = pltpu.VMEM((ext, slots, slots), BF)
    scratch_d = [lhs_scratch, pltpu.VMEM((cells, KDIM, slots), BF), pltpu.VMEM((cells, 8, slots), F32)]
    scratch_f = [
        lhs_scratch,
        pltpu.VMEM((cells, KDIM, 2 * slots), BF),
        pltpu.VMEM((cells, 4, 8, slots), F32),
        pltpu.VMEM((ext, 3, slots, slots), F32),
    ]
    emb_shape = [shaped(planes, gy, gz, slots), shaped(1, gy, gz, slots), shaped(1, gy, gz, slots)]
    vec, edge = shaped(3, planes, gy, gz, slots), shaped(3, 1, gy, gz, slots)
    pack = shaped(6, 1, gy, gz, slots)
    number = [smem] * 3
    cost_d = pl.CostEstimate(flops=pairs * 10, bytes_accessed=2**20, transcendentals=0)
    cost_f = pl.CostEstimate(flops=pairs * 25, bytes_accessed=2**20, transcendentals=0)

    held, hops = None, exit_hops(lax.axis_size("rep"))
    me, chosen = lax.axis_index("rep"), exit_replica[0]

    def hop(index, held):
        stride, radix = hops[index]
        digit, root = (me // stride) % radix, (chosen // stride) % radix
        options = [held]
        for turn in range(1, radix):
            pairs = []
            for i in range(lax.axis_size("rep")):
                at = (i // stride) % radix
                pairs.append((i, i + (((at + turn) % radix) - at) * stride))
            options.append(lax.ppermute(held, "rep", pairs))
        return options, (digit - root) % radix

    motion = start_vel
    coords = (pos_lo, start_pos, pos_hi)
    for quench_step in range(QUENCH):
        args = [*coords, count_lo, counts, count_hi]
        specs = [vmem] * 3 + number
        if quench_step == 0:
            emb, emb_first, emb_last, blocks = pl.pallas_call(
                functools.partial(density_kernel, dims, True),
                out_shape=(*emb_shape, jax.ShapeDtypeStruct((entries,), jnp.int32)),
                in_specs=specs + [smem, smem],
                out_specs=(vmem, vmem, vmem, smem),
                scratch_shapes=scratch_d,
                compiler_params=pltpu.CompilerParams(vmem_limit_bytes=12 * 2**20),
                cost_estimate=cost_d,
                name="density_first",
            )(*args, pair_flags, flags_lo)
        else:
            emb, emb_first, emb_last, *coords, motion = pl.pallas_call(
                functools.partial(density_kernel, dims, False),
                out_shape=(*emb_shape, edge, vec, edge, vec),
                in_specs=specs + [smem] + [vmem] * (4 + space),
                out_specs=(vmem,) * 7,
                scratch_shapes=scratch_d,
                compiler_params=pltpu.CompilerParams(vmem_limit_bytes=12 * 2**20),
                cost_estimate=cost_d,
                name="density_next",
            )(*args, blocks, forces, pushed, *packs, *sums)
            args = [*coords, count_lo, counts, count_hi]
        emb_lo, emb_hi = halo(emb_first, emb_last)
        last = quench_step == QUENCH - 1
        forces, pushed, part, *edges = pl.pallas_call(
            functools.partial(force_kernel, dims),
            out_shape=(vec, vec, shaped(8, slots), *(() if last else (pack, pack))),
            in_specs=specs + [vmem] * 4 + [smem],
            out_specs=(vmem,) * (3 if last else 5),
            scratch_shapes=scratch_f,
            compiler_params=pltpu.CompilerParams(vmem_limit_bytes=42 * 2**20),
            cost_estimate=cost_f,
            name="force",
        )(*args, emb_lo, emb, emb_hi, motion, blocks)
        sums = [part] + [lax.ppermute(part, "space", ring("space", s)) for s in range(1, space)]
        if not last:
            packs = halo(*edges)
        if quench_step == 0:
            held = jnp.concatenate([start_pos, pushed], axis=0)
            for index in range(len(hops) - 1):
                options, pick = hop(index, held)
                held = options[0]
                for turn in range(1, len(options)):
                    held = jnp.where(pick == turn, options[turn], held)
            options, pick = hop(len(hops) - 1, held)

    quench_pos, quench_vel, place, drift = pl.pallas_call(
        functools.partial(finish_kernel, dims, len(options)),
        out_shape=(vec,) * 4,
        in_specs=[vmem] * 4 + [smem] * 2 + [vmem] * (len(options) + space),
        out_specs=(vmem,) * 4,
        compiler_params=pltpu.CompilerParams(vmem_limit_bytes=12 * 2**20),
        name="finish",
    )(coords[1], forces, pushed, thermal_noise[0, 0], counts, pick[None], *options, *sums)
    return quench_pos[None], quench_vel[None], place[None], drift[None]


def solution(mesh):
    vector = P("rep", None, "space", None, None, None)
    placed = (
        vector,
        vector,
        P("rep", None, None, "space", None, None, None),
        P("space", None, None),
        P(None, "space", None, None),
        P(),
    )
    return jax.shard_map(body, mesh=mesh, in_specs=placed, out_specs=(vector,) * 4, check_vma=False)
```

```python
import functools
import math

import jax
import jax.numpy as jnp
from jax import lax
from jax.experimental import pallas as pl
from jax.experimental.pallas import tpu as pltpu
from jax.sharding import PartitionSpec as P


QUENCH = 2
STEP_SIZE = 0.1
ALPHA_MIX = 0.25
EPSILON = 1e-06
FRICTION = math.exp(-0.2)
KICK_SCALE = math.sqrt(1.0 - FRICTION * FRICTION)
HALF_OFFSETS = (
    [(1, p, q) for p in (-1, 0, 1) for q in (-1, 0, 1)]
    + [(0, 1, q) for q in (-1, 0, 1)]
    + [(0, 0, 1)]
)
OFFSETS = [(i, j, k) for i in (-1, 0, 1) for j in (-1, 0, 1) for k in (-1, 0, 1)]
FAR = 1.0e6
BF = jnp.bfloat16
F32 = jnp.float32
KDIM = 64
TILE = 32
ITEM = 12
GROUP = 4


def ring(axis, shift):
    count = lax.axis_size(axis)
    return [(i, (i + shift) % count) for i in range(count)]


def flag_of(offset):
    for index, entry in enumerate(HALF_OFFSETS):
        if entry == offset:
            return index, True
        if entry == tuple(-v for v in offset):
            return index, False
    return None


def rows_of(cell, slots):
    if isinstance(cell, int):
        return pl.ds(cell * slots, slots)
    return pl.ds(pl.multiple_of(cell * slots, slots), slots)


def split3(value):
    high = value.astype(BF).astype(F32)
    rest = value - high
    mid = rest.astype(BF).astype(F32)
    return high, mid, (rest - mid).astype(BF).astype(F32)


def wrap(index, size):
    index = jnp.where(index < 0, index + size, index)
    return jnp.where(index >= size, index - size, index)


def list_sizes(dims, slots):
    most = math.prod(dims) * -(-27 * (slots // TILE) // ITEM)
    head = 8
    return head, most + 2 * GROUP, head + (most + 2 * GROUP) * (ITEM + 1) + 2 * ITEM


class ListBuilder:
    def __init__(self, dims, slots, cnt, flags, flags_lo, list_ref, size_ref):
        self.dims, self.slots, self.flags, self.flags_lo = dims, slots, flags, flags_lo
        self.list_ref, self.size_ref = list_ref, size_ref
        planes, gy, gz = dims
        self.head, items, _ = list_sizes(dims, slots)
        self.entries = self.head + items
        self.dummy = (planes + 2) * (gy + 2) * (gz + 2) * slots
        cells = [(p, z) for p in range(planes) for z in range(gz)]
        self.shares = [cells[j :: planes + 2] for j in range(planes + 2)]
        for j in range(planes + 2):
            which, at = (0, 0) if j == 0 else ((2, 0) if j == planes + 1 else (1, j - 1))

            def row(y, _):
                for z in range(gz):
                    size_ref[(j * gy + y) * gz + z] = (cnt[which][at, y, z] + (TILE - 1)) >> (
                        TILE.bit_length() - 1
                    )
                return 0

            lax.fori_loop(0, gy, row, 0)

    def add_cell(self, p, y, z, item):
        _, gy, gz = self.dims
        ey, ez = gy + 2, gz + 2
        at = self.entries + item * ITEM
        for ox, oy, oz in OFFSETS:
            ext = ((p + 1 + ox) * ey + (y + 1 + oy)) * ez + (z + 1 + oz)
            jy, jz = wrap(y + oy, gy), (z + oz) % gz
            number = self.size_ref[((p + 1 + ox) * gy + jy) * gz + jz]
            for t in range(self.slots // TILE):
                self.list_ref[at + t] = ext * self.slots + t * TILE
            found = flag_of((ox, oy, oz))
            if found is not None:
                index, forward = found
                if forward:
                    flag = self.flags[index, p, y, z]
                elif p + ox < 0:
                    flag = self.flags_lo[index, 0, jy, jz]
                else:
                    flag = self.flags[index, p + ox, jy, jz]
                number = number * flag
            at = at + number
        for t in range(ITEM):
            self.list_ref[at + t] = self.dummy
        for t in range(-(-27 * (self.slots // TILE) // ITEM)):
            self.list_ref[self.head + item + t] = (p * gy + y) * gz + z
        return lax.div(at - self.entries + (ITEM - 1), jnp.int32(ITEM))

    def add_row(self, j, y, item):
        for p, z in self.shares[j]:
            item = self.add_cell(p, y, z, item)
        return item

    def close(self, item):
        self.list_ref[0] = (item + (GROUP - 1)) // GROUP * GROUP
        last = self.list_ref[self.head + item - 1]

        def rest(i, _):
            self.list_ref[self.head + item + i] = last
            for t in range(ITEM):
                self.list_ref[self.entries + (item + i) * ITEM + t] = self.dummy
            return 0

        lax.fori_loop(0, 2 * GROUP - 1, rest, 0)


def build_partners(dims, pos, cnt, emb, lister, lhs_ref, wide_ref, *accs):
    planes, gy, gz = dims
    ey, ez = gy + 2, gz + 2
    slots = lhs_ref.shape[-1]
    full = (8, slots)
    rows = lax.broadcasted_iota(jnp.int32, full, 0)
    lane = lax.broadcasted_iota(jnp.int32, full, 1)
    blank = jnp.zeros((slots - KDIM, slots), F32)

    def store(ext, value):
        h, m, l = split3(value)
        tall = jnp.concatenate([h, h, h, m, m, m, l, l, blank], axis=0).T.astype(BF)
        lhs_ref[rows_of(ext, slots), :] = tall
        return tall

    if wide_ref is not None:
        row = lax.broadcasted_iota(jnp.int32, (2 * slots, 2 * slots), 0)
        col = lax.broadcasted_iota(jnp.int32, (2 * slots, 2 * slots), 1) // slots
        line_row = row % slots
        used = (line_row < 8) | ((line_row >= 24) & (line_row < 32)) | ((line_row >= 48) & (line_row < 56))
        side = jnp.zeros((slots, slots), BF)
        half = slots // 2
        acc_xy, acc_z = accs[:gz], accs[gz:]
        for m in range(2):
            if m == 0:
                chosen = used & (row < slots) & (line_row % 8 == col)
            else:
                chosen = used & (row // slots == col) & (line_row % 8 == 2)
            pick = jnp.where(chosen, 1.0, 0.0)
            pltpu.matmul_push_rhs(pick.astype(BF), staging_register=0, mxu_index=m)
        for m in range(2):
            for index, acc in enumerate((acc_xy, acc_z)[m]):
                pltpu.matmul_acc_lhs(
                    acc,
                    jnp.zeros((slots if m == 0 else half, 2 * slots), BF),
                    load_staged_rhs=0 if index == 0 else None,
                )

    def one(j, which, at, y, z, by, bz):
        raw = [
            jnp.broadcast_to(pos[which][k, at, by, pl.ds(bz, 1), :], full) for k in range(3)
        ]
        xx = raw[0] + (j - 0.5 - (planes + 1) / 2)
        yy = raw[1] + (jnp.asarray(y).astype(F32) - 0.5 - (gy + 1) / 2)
        zz = raw[2] + (z - 0.5 - (gz + 1) / 2)
        norm = xx * xx + yy * yy + zz * zz
        norm = jnp.where(lane < cnt[which][at, by, bz], norm, norm + FAR)
        value = jnp.where(rows == 0, xx, jnp.where(rows == 1, yy, zz))
        value = jnp.where(rows == 3, norm, value)
        value = jnp.where(rows >= 4, 1.0, value)
        if emb is not None:
            e = jnp.broadcast_to(emb[which][at, by, pl.ds(bz, 1), :], full) * 0.25
            value = jnp.where(rows == 6, e, value)
        return store((j * ey + y) * ez + z, value)

    def put(spot):
        for z in range(1, gz + 1):
            both = pltpu.matmul_pop(acc_xy[z - 1])
            for at in [z] + [0] * (z == gz) + [gz + 1] * (z == 1):
                wide_ref[0, rows_of(spot + at, slots), :] = both[:, :slots]
                wide_ref[1, rows_of(spot + at, slots), :] = both[:, slots:]
        for z in range(ez):
            both = pltpu.matmul_pop(acc_z[z])
            wide_ref[2, rows_of(spot + z, slots), :] = jnp.concatenate(
                [both[:, :slots], both[:, slots:]], axis=0
            )

    spot, item = jnp.int32(0), jnp.int32(0)
    for j in range(planes + 2):
        which, at = (0, 0) if j == 0 else ((2, 0) if j == planes + 1 else (1, j - 1))

        def line(y, spot):
            by = wrap(y - 1, gy)
            talls = [one(j, which, at, y, z, by, (z - 1) % gz) for z in range(ez)]
            if wide_ref is None:
                return spot
            put(spot)
            for z in range(ez):
                if 1 <= z <= gz:
                    pltpu.matmul_acc_lhs(acc_xy[z - 1], jnp.concatenate([talls[z], side], axis=1))
                pltpu.matmul_acc_lhs(
                    acc_z[z], jnp.concatenate([talls[z][:half], talls[z][half:]], axis=1)
                )
            return (j * ey + y) * ez

        def line_and_list(y, item):
            line(y, None)
            return lister.add_row(j, y, item)

        if lister is None:
            spot = lax.fori_loop(0, ey, line, spot)
        else:
            item = lax.fori_loop(0, gy, line_and_list, item)
            lax.fori_loop(gy, ey, lambda y, zero: line(y, None) or zero, 0)
    if lister is not None:
        lister.close(item)
    if wide_ref is not None:
        put(spot)
        for k in range(3):
            wide_ref[k, (planes + 2) * ey * ez * slots :, :] = jnp.zeros((slots, slots), F32)
    store((planes + 2) * ey * ez, jnp.where(rows == 3, FAR, jnp.where(rows >= 4, 1.0, 0.0)))


def build_center(dims, p, y, z, x3, count, e_row):
    planes, gy, gz = dims
    slots = x3[0].shape[-1]
    full = (8, slots)
    rows = lax.broadcasted_iota(jnp.int32, full, 0)
    lane = lax.broadcasted_iota(jnp.int32, full, 1)
    xx = jnp.broadcast_to(x3[0], full) + (p + 0.5 - (planes + 1) / 2)
    yy = jnp.broadcast_to(x3[1], full) + (y.astype(F32) + 0.5 - (gy + 1) / 2)
    zz = jnp.broadcast_to(x3[2], full) + (z.astype(F32) + 0.5 - (gz + 1) / 2)
    one = 1.0 - (xx * xx + yy * yy + zz * zz)
    one = jnp.where(lane < count, one, one - FAR)
    value = jnp.where(rows == 0, xx, jnp.where(rows == 1, yy, zz)) * 2.0
    value = jnp.where(rows == 4, one, value)
    if e_row is not None:
        value = jnp.where(rows == 5, jnp.broadcast_to(e_row, full) * 0.25, value)
    parts = split3(value)
    us, ws = [], []
    for block in range(8):
        part = parts[block % 3]
        keep = rows < 3
        if block < 3:
            keep = keep | (rows == 4)
        u = jnp.where(keep, part, 0.0)
        if block % 3 == 0:
            u = jnp.where(rows == 3, -1.0, u)
        us.append(u)
        if e_row is not None:
            w = u
            if block < 3:
                w = jnp.where(rows == 5, part, w)
            if block % 3 == 0:
                w = jnp.where(rows == 6, 1.0, w)
            ws.append(w)
    right = jnp.concatenate(us, axis=0).astype(BF)
    if e_row is None:
        return right
    return jnp.concatenate([right, jnp.concatenate(ws, axis=0).astype(BF)], axis=1)


def mix_factor(sum_refs):
    total = sum_refs[0][...]
    for ref in sum_refs[1:]:
        total = total + ref[...]
    force_sq = jnp.sum(total[0:1], axis=1, keepdims=True)
    vel_sq = jnp.sum(total[1:2], axis=1, keepdims=True)
    return jnp.sqrt(vel_sq / (force_sq + EPSILON))


def quench_update(dims, mix, x_ref, f_of, v_of, planes, x_out, v_out):
    gy, _ = dims[1:]
    for k in range(3):
        for p in range(planes):
            for y in range(gy):
                v = (1.0 - ALPHA_MIX) * v_of(k, p, y) + ALPHA_MIX * mix * f_of(k, p, y)
                if v_out is not None:
                    v_out[k, p, y] = v
                x_out[k, p, y] = x_ref[k, p, y] + STEP_SIZE * v


def density_kernel(dims, first, *refs):
    planes, gy, gz = dims
    if first:
        (p0, p1, p2, c0, c1, c2, fl, fl_lo, emb_ref, lo_ref, hi_ref, list_ref, lhs_ref, right_ref, res_ref, size_ref) = refs
        lister = ListBuilder(dims, lhs_ref.shape[-1], (c0, c1, c2), fl, fl_lo, list_ref, size_ref)
    else:
        (q0, q1, q2, c0, c1, c2, list_ref, f_ref, v_ref, b0, b2) = refs[:11]
        sum_refs = refs[11:-10]
        (emb_ref, lo_ref, hi_ref, p0, p1, p2, v_out, lhs_ref, right_ref, res_ref) = refs[-10:]
        lister = None
        mix = mix_factor(sum_refs)
        quench_update(
            dims, mix, q1, lambda k, p, y: f_ref[k, p, y], lambda k, p, y: v_ref[k, p, y], planes, p1, v_out
        )
        for q, b, out in ((q0, b0, p0), (q2, b2, p2)):
            quench_update(
                dims, mix, q, lambda k, p, y, b=b: b[k, p, y], lambda k, p, y, b=b: b[k + 3, p, y], 1, out, None
            )
    slots = lhs_ref.shape[-1]
    build_partners(dims, (p0, p1, p2), (c0, c1, c2), None, lister, lhs_ref, None)
    build_rights(dims, p1, c1, None, right_ref)
    gap = jnp.zeros((slots - KDIM, slots), BF)
    side = jnp.zeros((slots, slots), BF)

    def right_of(cell):
        one = jnp.concatenate([right_ref[cell], gap], axis=0)
        return jnp.concatenate(
            [jnp.concatenate([one, side], axis=1), jnp.concatenate([side, one], axis=1)], axis=0
        )

    def left_of(starts):
        return jnp.concatenate([lhs_ref[tile_at(start), :] for start in starts], axis=1)

    def work(starts, value, acc):
        for r in range(TILE // 8):
            for h in range(2):
                t = jnp.maximum(value[r * 8 : r * 8 + 8, h * slots : (h + 1) * slots], 0.0)
                acc[r % 4] = acc[r % 4] + t * t * t

    def emit(cell, acc):
        res_ref[cell] = (acc[0] + acc[1]) + (acc[2] + acc[3])

    run_items(dims, slots, list_ref, GROUP, 2, 4, right_of, left_of, work, emit)
    lane = lax.broadcasted_iota(jnp.int32, (1, slots), 1)
    for p in range(planes):

        def row(y, _):
            for z in range(gz):
                total = jnp.sum(res_ref[(p * gy + y) * gz + z], axis=0, keepdims=True)
                total = total - jnp.where(lane < c1[p, y, z], 1.0, 0.0)
                emb = -lax.rsqrt(1.0 + total / slots)
                emb_ref[p, y, z : z + 1, :] = emb
                if p == 0:
                    lo_ref[0, y, z : z + 1, :] = emb
                if p == planes - 1:
                    hi_ref[0, y, z : z + 1, :] = emb
            return 0

        lax.fori_loop(0, gy, row, 0)


def build_rights(dims, pos, cnt, emb, right_ref):
    planes, gy, gz = dims
    for p in range(planes):

        def row(y, _):
            for z in range(gz):
                x3 = [pos[k, p, y, z : z + 1, :] for k in range(3)]
                e_row = None if emb is None else emb[p, y, z : z + 1, :]
                right_ref[(p * gy + y) * gz + z] = build_center(
                    dims, p, y, jnp.int32(z), x3, cnt[p, y, z], e_row
                )
            return 0

        lax.fori_loop(0, gy, row, 0)


def tile_at(start):
    return pl.ds(pl.multiple_of(start, TILE), TILE)


def run_items(dims, slots, list_ref, group, width, chains, right_of, left_of, work, emit):
    head, items, _ = list_sizes(dims, slots)
    entries = head + items
    turns = ITEM // (2 * width)

    def inner(*flat):
        accs = [
            [[flat[(i * 2 + m) * turns + t] for t in range(turns)] for m in range(2)]
            for i in range(group)
        ]

        def starts_of(item, m, t):
            return [list_ref[entries + item * ITEM + (t * 2 + m) * width + w] for w in range(width)]

        def load_right(item):
            right = right_of(list_ref[head + item])
            for m in range(2):
                pltpu.matmul_push_rhs(right, staging_register=0, mxu_index=m)

        def send(item, i, m, t):
            pltpu.matmul_acc_lhs(
                accs[i][m][t],
                left_of(starts_of(item, m, t)),
                load_staged_rhs=0 if t == 0 else None,
            )

        for i in range(group):
            load_right(i)
            for t in range(turns):
                for m in range(2):
                    send(i, i, m, t)

        def step(turn, carry):
            acc = list(carry)
            for i in range(group):
                item = turn * group + i
                cell = list_ref[head + item]
                same = cell == list_ref[head + jnp.maximum(item - 1, 0)]
                keep = same.astype(F32)
                acc = [value * keep for value in acc]
                load_right(item + group)
                for t in range(turns):
                    for m in range(2):
                        value = pltpu.matmul_pop(accs[i][m][t])
                        send(item + group, i, m, t)
                        work(starts_of(item, m, t), value, acc)
                emit(cell, acc)
            return tuple(acc)

        zero = jnp.zeros((8, slots), F32)
        lax.fori_loop(0, list_ref[0] // group, step, (zero,) * chains)
        for i in range(group):
            for t in range(turns):
                for m in range(2):
                    pltpu.matmul_pop(accs[i][m][t])

    pl.run_scoped(
        inner,
        *[
            pltpu.ACC(m)((TILE, 2 * slots), F32)
            for _ in range(group)
            for m in range(2)
            for _ in range(turns)
        ],
    )


def force_kernel(dims, *refs):
    (p0, p1, p2, c0, c1, c2, e0, e1, e2, vel, list_ref) = refs[:11]
    (f_ref, v_ref, s_ref) = refs[11:14]
    edges = refs[14:-4]
    (lhs_ref, right_ref, res_ref, wide_ref) = refs[-4:]
    planes, gy, gz = dims
    slots = lhs_ref.shape[-1]
    pl.run_scoped(
        functools.partial(build_partners, dims, (p0, p1, p2), (c0, c1, c2), (e0, e1, e2), None, lhs_ref, wide_ref),
        *[pltpu.ACC(0)((slots, 2 * slots), F32) for _ in range(gz)],
        *[pltpu.ACC(1)((slots // 2, 2 * slots), F32) for _ in range(gz + 2)],
    )
    build_rights(dims, p1, c1, e1, right_ref)
    gap = jnp.zeros((2 * slots - KDIM, 2 * slots), BF)
    side = jnp.zeros((TILE, slots), BF)

    def right_of(cell):
        return jnp.concatenate([right_ref[cell], gap], axis=0)

    def left_of(starts):
        return jnp.concatenate([lhs_ref[tile_at(starts[0]), :], side], axis=1)

    def work(starts, value, acc):
        wides = [wide_ref[k, tile_at(starts[0]), :] for k in range(3)]
        for r in range(TILE // 8):
            here = slice(r * 8, r * 8 + 8)
            t = jnp.maximum(value[here, :slots], 0.0)
            g = t * t * value[here, slots:]
            at = (r % 2) * 4
            acc[at] = acc[at] + g
            for k in range(3):
                acc[at + 1 + k] = acc[at + 1 + k] + g * wides[k][here]

    def emit(cell, acc):
        for k in range(4):
            res_ref[cell, k] = acc[k] + acc[k + 4]

    run_items(dims, slots, list_ref, 2, 1, 8, right_of, left_of, work, emit)
    lane = lax.broadcasted_iota(jnp.int32, (1, slots), 1)
    sums = (jnp.zeros((1, slots), F32), jnp.zeros((1, slots), F32))
    for p in range(planes):

        def row(y, sums):
            ff, vv = sums
            for z in range(gz):
                cell = (p * gy + y) * gz + z
                one = slice(z, z + 1)
                center = (
                    p + 0.5 - (planes + 1) / 2,
                    y.astype(F32) + 0.5 - (gy + 1) / 2,
                    z + 0.5 - (gz + 1) / 2,
                )
                total = jnp.sum(res_ref[cell, 0], axis=0, keepdims=True)
                for k in range(3):
                    x = p1[k, p, y, one, :] + center[k]
                    f = (24.0 / slots) * (x * total - jnp.sum(res_ref[cell, k + 1], axis=0, keepdims=True))
                    f_ref[k, p, y, one, :] = f
                    v = jnp.where(lane < c1[p, y, z], vel[k, p, y, one, :], 0.0) + STEP_SIZE * f
                    v_ref[k, p, y, one, :] = v
                    if edges and p == 0:
                        edges[0][k, 0, y, one, :] = f
                        edges[0][k + 3, 0, y, one, :] = v
                    if edges and p == planes - 1:
                        edges[1][k, 0, y, one, :] = f
                        edges[1][k + 3, 0, y, one, :] = v
                    ff = ff + f * f
                    vv = vv + v * v
            return ff, vv

        sums = lax.fori_loop(0, gy, row, sums)
    s_ref[...] = jnp.concatenate([sums[0], sums[1], jnp.zeros((6, slots), F32)], axis=0)


def finish_kernel(dims, radix, *refs):
    (x_ref, f_ref, v_ref, noise, cnt, pick) = refs[:6]
    options = refs[6 : 6 + radix]
    sum_refs = refs[6 + radix : -4]
    (xq, vq, xd, vd) = refs[-4:]
    planes, gy, gz = dims
    slots = x_ref.shape[-1]
    mix = mix_factor(sum_refs)
    quench_update(
        dims, mix, x_ref, lambda k, p, y: f_ref[k, p, y], lambda k, p, y: v_ref[k, p, y], planes, xq, vq
    )
    lane = lax.broadcasted_iota(jnp.int32, (gz, slots), 1)
    line = lax.broadcasted_iota(jnp.int32, (gz, slots), 0)
    take = pick[0]
    for p in range(planes):
        for y in range(gy):
            limit = jnp.zeros((gz, slots), jnp.int32)
            for z in range(gz):
                limit = jnp.where(line == z, cnt[p, y, z], limit)
            occupied = (lane < limit).astype(F32)
            for k in range(3):
                place, push = options[0][k, p, y], options[0][k + 3, p, y]
                for index in range(1, radix):
                    place = jnp.where(take == index, options[index][k, p, y], place)
                    push = jnp.where(take == index, options[index][k + 3, p, y], push)
                v = FRICTION * push + KICK_SCALE * occupied * noise[k, p, y]
                vd[k, p, y] = v
                xd[k, p, y] = place + STEP_SIZE * v


def exit_hops(count):
    hops, stride = [], 1
    while stride < count:
        left = count // stride
        radix = next(r for r in (4, 2, 3, 5, 7, left) if left % r == 0)
        hops.append((stride, radix))
        stride *= radix
    return hops


def body(positions, velocities, thermal_noise, counts, pair_flags, exit_replica):
    start_pos = positions[0]
    start_vel = velocities[0]
    planes, gy, gz, slots = start_pos.shape[1:]
    dims = (planes, gy, gz)
    up, down = ring("space", 1), ring("space", -1)
    space = lax.axis_size("space")
    vmem = pl.BlockSpec(memory_space=pltpu.VMEM)
    smem = pl.BlockSpec(memory_space=pltpu.SMEM)
    ext = (planes + 2) * (gy + 2) * (gz + 2) + 1
    cells = planes * gy * gz
    entries = list_sizes(dims, slots)[2]
    pairs = planes * gy * gz * 27 * slots * slots

    def shaped(*shape):
        return jax.ShapeDtypeStruct(shape, F32)

    def planes_of(block, dim):
        return lax.slice_in_dim(block, 0, 1, axis=dim), lax.slice_in_dim(block, planes - 1, planes, axis=dim)

    def halo(first, last):
        return lax.ppermute(last, "space", up), lax.ppermute(first, "space", down)

    flags_lo = lax.ppermute(lax.slice_in_dim(pair_flags, planes - 1, planes, axis=1), "space", up)
    count_lo, count_hi = halo(*planes_of(counts, 0))
    pos_lo, pos_hi = halo(*planes_of(start_pos, 1))
    lhs_scratch = pltpu.VMEM((ext * slots, slots), BF)
    scratch_d = [lhs_scratch, pltpu.VMEM((cells, KDIM, slots), BF), pltpu.VMEM((cells, 8, slots), F32)]
    scratch_f = [
        lhs_scratch,
        pltpu.VMEM((cells, KDIM, 2 * slots), BF),
        pltpu.VMEM((cells, 4, 8, slots), F32),
        pltpu.VMEM((3, ext * slots, slots), F32),
    ]
    emb_shape = [shaped(planes, gy, gz, slots), shaped(1, gy, gz, slots), shaped(1, gy, gz, slots)]
    vec, edge = shaped(3, planes, gy, gz, slots), shaped(3, 1, gy, gz, slots)
    pack = shaped(6, 1, gy, gz, slots)
    number = [smem] * 3
    cost_d = pl.CostEstimate(flops=pairs * 10, bytes_accessed=2**20, transcendentals=0)
    cost_f = pl.CostEstimate(flops=pairs * 25, bytes_accessed=2**20, transcendentals=0)

    held, hops = None, exit_hops(lax.axis_size("rep"))
    me, chosen = lax.axis_index("rep"), exit_replica[0]

    def hop(index, held):
        stride, radix = hops[index]
        digit, root = (me // stride) % radix, (chosen // stride) % radix
        options = [held]
        for turn in range(1, radix):
            pairs = []
            for i in range(lax.axis_size("rep")):
                at = (i // stride) % radix
                pairs.append((i, i + (((at + turn) % radix) - at) * stride))
            options.append(lax.ppermute(held, "rep", pairs))
        return options, (digit - root) % radix

    motion = start_vel
    coords = (pos_lo, start_pos, pos_hi)
    for quench_step in range(QUENCH):
        args = [*coords, count_lo, counts, count_hi]
        specs = [vmem] * 3 + number
        if quench_step == 0:
            emb, emb_first, emb_last, blocks = pl.pallas_call(
                functools.partial(density_kernel, dims, True),
                out_shape=(*emb_shape, jax.ShapeDtypeStruct((entries,), jnp.int32)),
                in_specs=specs + [smem, smem],
                out_specs=(vmem, vmem, vmem, smem),
                scratch_shapes=scratch_d + [pltpu.SMEM(((planes + 2) * gy * gz,), jnp.int32)],
                compiler_params=pltpu.CompilerParams(vmem_limit_bytes=12 * 2**20),
                cost_estimate=cost_d,
                name="density_first",
            )(*args, pair_flags, flags_lo)
        else:
            emb, emb_first, emb_last, *coords, motion = pl.pallas_call(
                functools.partial(density_kernel, dims, False),
                out_shape=(*emb_shape, edge, vec, edge, vec),
                in_specs=specs + [smem] + [vmem] * (4 + space),
                out_specs=(vmem,) * 7,
                scratch_shapes=scratch_d,
                compiler_params=pltpu.CompilerParams(vmem_limit_bytes=12 * 2**20),
                cost_estimate=cost_d,
                name="density_next",
            )(*args, blocks, forces, pushed, *packs, *sums)
            args = [*coords, count_lo, counts, count_hi]
        emb_lo, emb_hi = halo(emb_first, emb_last)
        last = quench_step == QUENCH - 1
        forces, pushed, part, *edges = pl.pallas_call(
            functools.partial(force_kernel, dims),
            out_shape=(vec, vec, shaped(8, slots), *(() if last else (pack, pack))),
            in_specs=specs + [vmem] * 4 + [smem],
            out_specs=(vmem,) * (3 if last else 5),
            scratch_shapes=scratch_f,
            compiler_params=pltpu.CompilerParams(vmem_limit_bytes=42 * 2**20),
            cost_estimate=cost_f,
            name="force",
        )(*args, emb_lo, emb, emb_hi, motion, blocks)
        sums = [part] + [lax.ppermute(part, "space", ring("space", s)) for s in range(1, space)]
        if not last:
            packs = halo(*edges)
        if quench_step == 0:
            held = jnp.concatenate([start_pos, pushed], axis=0)
            for index in range(len(hops) - 1):
                options, pick = hop(index, held)
                held = options[0]
                for turn in range(1, len(options)):
                    held = jnp.where(pick == turn, options[turn], held)
            options, pick = hop(len(hops) - 1, held)

    quench_pos, quench_vel, place, drift = pl.pallas_call(
        functools.partial(finish_kernel, dims, len(options)),
        out_shape=(vec,) * 4,
        in_specs=[vmem] * 4 + [smem] * 2 + [vmem] * (len(options) + space),
        out_specs=(vmem,) * 4,
        compiler_params=pltpu.CompilerParams(vmem_limit_bytes=12 * 2**20),
        name="finish",
    )(coords[1], forces, pushed, thermal_noise[0, 0], counts, pick[None], *options, *sums)
    return quench_pos[None], quench_vel[None], place[None], drift[None]


def solution(mesh):
    vector = P("rep", None, "space", None, None, None)
    placed = (
        vector,
        vector,
        P("rep", None, None, "space", None, None, None),
        P("space", None, None),
        P(None, "space", None, None),
        P(),
    )
    return jax.shard_map(body, mesh=mesh, in_specs=placed, out_specs=(vector,) * 4, check_vma=False)
```

```python
import functools
import math

import jax
import jax.numpy as jnp
from jax import lax
from jax.experimental import pallas as pl
from jax.experimental.pallas import tpu as pltpu
from jax.sharding import PartitionSpec as P


QUENCH = 2
STEP_SIZE = 0.1
ALPHA_MIX = 0.25
EPSILON = 1e-06
FRICTION = math.exp(-0.2)
KICK_SCALE = math.sqrt(1.0 - FRICTION * FRICTION)
HALF_OFFSETS = (
    [(1, p, q) for p in (-1, 0, 1) for q in (-1, 0, 1)]
    + [(0, 1, q) for q in (-1, 0, 1)]
    + [(0, 0, 1)]
)
OFFSETS = [(i, j, k) for i in (-1, 0, 1) for j in (-1, 0, 1) for k in (-1, 0, 1)]
FAR = 1.0e6
BF = jnp.bfloat16
F32 = jnp.float32
KDIM = 64
TILE = 32
ITEM = 12
GROUP = 4


def ring(axis, shift):
    count = lax.axis_size(axis)
    return [(i, (i + shift) % count) for i in range(count)]


def flag_of(offset):
    for index, entry in enumerate(HALF_OFFSETS):
        if entry == offset:
            return index, True
        if entry == tuple(-v for v in offset):
            return index, False
    return None


def rows_of(cell, slots):
    if isinstance(cell, int):
        return pl.ds(cell * slots, slots)
    return pl.ds(pl.multiple_of(cell * slots, slots), slots)


def split3(value):
    high = value.astype(BF).astype(F32)
    rest = value - high
    mid = rest.astype(BF).astype(F32)
    return high, mid, (rest - mid).astype(BF).astype(F32)


def wrap(index, size):
    index = jnp.where(index < 0, index + size, index)
    return jnp.where(index >= size, index - size, index)


def list_sizes(dims, slots):
    most = math.prod(dims) * -(-27 * (slots // TILE) // ITEM)
    head = 8
    return head, most + 2 * GROUP, head + (most + 2 * GROUP) * (ITEM + 1) + 2 * ITEM


class ListBuilder:
    def __init__(self, dims, slots, cnt, flags, flags_lo, list_ref, size_ref):
        self.dims, self.slots, self.flags, self.flags_lo = dims, slots, flags, flags_lo
        self.list_ref, self.size_ref = list_ref, size_ref
        planes, gy, gz = dims
        self.head, items, _ = list_sizes(dims, slots)
        self.entries = self.head + items
        self.dummy = (planes + 2) * (gy + 2) * (gz + 2) * slots
        cells = [(p, z) for p in range(planes) for z in range(gz)]
        self.shares = [cells[j :: planes + 2] for j in range(planes + 2)]
        for j in range(planes + 2):
            which, at = (0, 0) if j == 0 else ((2, 0) if j == planes + 1 else (1, j - 1))

            def row(y, _):
                for z in range(gz):
                    size_ref[(j * gy + y) * gz + z] = (cnt[which][at, y, z] + (TILE - 1)) >> (
                        TILE.bit_length() - 1
                    )
                return 0

            lax.fori_loop(0, gy, row, 0)

    def add_cell(self, p, y, z, item, base, near, spots):
        _, gy, gz = self.dims
        ey, ez = gy + 2, gz + 2
        at = self.entries + item * ITEM
        for ox, oy, oz in OFFSETS:
            first = (((p + 1 + ox) * ey + 1 + oy) * ez + (z + 1 + oz)) * self.slots
            jz = (z + oz) % gz
            number = self.size_ref[spots[oy] + ((p + 1 + ox) * gy * gz + jz)]
            for t in range(self.slots // TILE):
                self.list_ref[at + t] = base + (first + t * TILE)
            found = flag_of((ox, oy, oz))
            if found is not None:
                index, forward = found
                if forward:
                    flag = self.flags[index, p, y, z]
                elif p + ox < 0:
                    flag = self.flags_lo[index, 0, near[oy], jz]
                else:
                    flag = self.flags[index, p + ox, near[oy], jz]
                number = number * flag
            at = at + number
        for t in range(ITEM):
            self.list_ref[at + t] = self.dummy
        for t in range(-(-27 * (self.slots // TILE) // ITEM)):
            self.list_ref[self.head + item + t] = y * gz + (p * gy * gz + z)
        return lax.div(at - self.entries + (ITEM - 1), jnp.int32(ITEM))

    def add_row(self, j, y, item):
        gy, gz = self.dims[1:]
        base = y * ((gz + 2) * self.slots)
        near = {oy: wrap(y + oy, gy) for oy in (-1, 0, 1)}
        spots = {oy: near[oy] * gz for oy in (-1, 0, 1)}
        for p, z in self.shares[j]:
            item = self.add_cell(p, y, z, item, base, near, spots)
        return item

    def close(self, item):
        self.list_ref[0] = (item + (GROUP - 1)) // GROUP * GROUP
        last = self.list_ref[self.head + item - 1]

        def rest(i, _):
            self.list_ref[self.head + item + i] = last
            for t in range(ITEM):
                self.list_ref[self.entries + (item + i) * ITEM + t] = self.dummy
            return 0

        lax.fori_loop(0, 2 * GROUP - 1, rest, 0)


def build_partners(dims, pos, cnt, emb, lister, lhs_ref, wide_ref, *accs):
    planes, gy, gz = dims
    ey, ez = gy + 2, gz + 2
    slots = lhs_ref.shape[-1]
    full = (8, slots)
    rows = lax.broadcasted_iota(jnp.int32, full, 0)
    lane = lax.broadcasted_iota(jnp.int32, full, 1)
    blank = jnp.zeros((slots - KDIM, slots), F32)

    def store(ext, value):
        h, m, l = split3(value)
        tall = jnp.concatenate([h, h, h, m, m, m, l, l, blank], axis=0).T.astype(BF)
        lhs_ref[rows_of(ext, slots), :] = tall
        return tall

    if wide_ref is not None:
        row = lax.broadcasted_iota(jnp.int32, (2 * slots, 2 * slots), 0)
        col = lax.broadcasted_iota(jnp.int32, (2 * slots, 2 * slots), 1) // slots
        line_row = row % slots
        used = (line_row < 8) | ((line_row >= 24) & (line_row < 32)) | ((line_row >= 48) & (line_row < 56))
        side = jnp.zeros((slots, slots), BF)
        half = slots // 2
        acc_xy, acc_z = accs[:gz], accs[gz:]
        for m in range(2):
            if m == 0:
                chosen = used & (row < slots) & (line_row % 8 == col)
            else:
                chosen = used & (row // slots == col) & (line_row % 8 == 2)
            pick = jnp.where(chosen, 1.0, 0.0)
            pltpu.matmul_push_rhs(pick.astype(BF), staging_register=0, mxu_index=m)
        for acc, height in ((acc_xy[0], slots), (acc_z[0], half)):
            pltpu.matmul_acc_lhs(acc, jnp.zeros((height, 2 * slots), BF), load_staged_rhs=0)
            pltpu.matmul_pop(acc)

    def one(j, which, at, y, z, by, bz):
        raw = [
            jnp.broadcast_to(pos[which][k, at, by, pl.ds(bz, 1), :], full) for k in range(3)
        ]
        xx = raw[0] + (j - 0.5 - (planes + 1) / 2)
        yy = raw[1] + (jnp.asarray(y).astype(F32) - 0.5 - (gy + 1) / 2)
        zz = raw[2] + (z - 0.5 - (gz + 1) / 2)
        norm = xx * xx + yy * yy + zz * zz
        norm = jnp.where(lane < cnt[which][at, by, bz], norm, norm + FAR)
        value = jnp.where(rows == 0, xx, jnp.where(rows == 1, yy, zz))
        value = jnp.where(rows == 3, norm, value)
        value = jnp.where(rows >= 4, 1.0, value)
        if emb is not None:
            e = jnp.broadcast_to(emb[which][at, by, pl.ds(bz, 1), :], full) * 0.25
            value = jnp.where(rows == 6, e, value)
        return store((j * ey + y) * ez + z, value)

    def put(spot, images=()):
        for z in range(1, gz + 1):
            both = pltpu.matmul_pop(acc_xy[z - 1])
            deep = pltpu.matmul_pop(acc_z[z - 1])
            deep = jnp.concatenate([deep[:, :slots], deep[:, slots:]], axis=0)
            wide_x, wide_y = both[:, :slots], both[:, slots:]
            for line, shift in ((spot, 0.0), *images):
                here = wide_y + shift if shift else wide_y
                for at, turn in [(z, 0.0)] + [(0, -1.0 * gz)] * (z == gz) + [(gz + 1, 1.0 * gz)] * (z == 1):
                    rows_at = rows_of(line + at, slots)
                    wide_ref[0, rows_at, :] = wide_x
                    wide_ref[1, rows_at, :] = here
                    wide_ref[2, rows_at, :] = deep + turn if turn else deep

    def send(talls):
        for z in range(1, gz + 1):
            pltpu.matmul_acc_lhs(acc_xy[z - 1], jnp.concatenate([talls[z], side], axis=1))
            pltpu.matmul_acc_lhs(acc_z[z - 1], jnp.concatenate([talls[z][:half], talls[z][half:]], axis=1))

    item = jnp.int32(0)
    for j in range(planes + 2):
        which, at = (0, 0) if j == 0 else ((2, 0) if j == planes + 1 else (1, j - 1))

        def line(y, by):
            return [one(j, which, at, y, z, by, (z - 1) % gz) for z in range(ez)]

        def wide_line(y, _):
            talls = line(y, y - 1)
            put((j * ey + y - 1) * ez)
            send(talls)
            return 0

        def line_and_list(y, item):
            line(y, wrap(y - 1, gy))
            return lister.add_row(j, y, item)

        def plain(y, _):
            line(y, wrap(y - 1, gy))
            return 0

        if wide_ref is not None:
            base = j * ey * ez
            line(0, gy - 1)
            send(line(1, 0))
            talls = line(2, 1)
            put(base + ez, [(base + (gy + 1) * ez, 1.0 * gy)])
            send(talls)
            lax.fori_loop(3, gy + 1, wide_line, 0)
            line(gy + 1, 0)
            put(base + gy * ez, [(base, -1.0 * gy)])
        elif lister is None:
            lax.fori_loop(0, ey, plain, 0)
        else:
            item = lax.fori_loop(0, gy, line_and_list, item)
            lax.fori_loop(gy, ey, plain, 0)
    if lister is not None:
        lister.close(item)
    if wide_ref is not None:
        for k in range(3):
            wide_ref[k, (planes + 2) * ey * ez * slots :, :] = jnp.zeros((slots, slots), F32)
    store((planes + 2) * ey * ez, jnp.where(rows == 3, FAR, jnp.where(rows >= 4, 1.0, 0.0)))


def build_center(dims, p, y, z, x3, count, e_row):
    planes, gy, gz = dims
    slots = x3[0].shape[-1]
    full = (8, slots)
    rows = lax.broadcasted_iota(jnp.int32, full, 0)
    lane = lax.broadcasted_iota(jnp.int32, full, 1)
    xx = jnp.broadcast_to(x3[0], full) + (p + 0.5 - (planes + 1) / 2)
    yy = jnp.broadcast_to(x3[1], full) + (y.astype(F32) + 0.5 - (gy + 1) / 2)
    zz = jnp.broadcast_to(x3[2], full) + (z.astype(F32) + 0.5 - (gz + 1) / 2)
    one = 1.0 - (xx * xx + yy * yy + zz * zz)
    one = jnp.where(lane < count, one, one - FAR)
    value = jnp.where(rows == 0, xx, jnp.where(rows == 1, yy, zz)) * 2.0
    value = jnp.where(rows == 4, one, value)
    if e_row is not None:
        value = jnp.where(rows == 5, jnp.broadcast_to(e_row, full) * 0.25, value)
    parts = split3(value)
    us, ws = [], []
    for block in range(8):
        part = parts[block % 3]
        keep = rows < 3
        if block < 3:
            keep = keep | (rows == 4)
        u = jnp.where(keep, part, 0.0)
        if block % 3 == 0:
            u = jnp.where(rows == 3, -1.0, u)
        us.append(u)
        if e_row is not None:
            w = u
            if block < 3:
                w = jnp.where(rows == 5, part, w)
            if block % 3 == 0:
                w = jnp.where(rows == 6, 1.0, w)
            ws.append(w)
    right = jnp.concatenate(us, axis=0).astype(BF)
    if e_row is None:
        return right
    return jnp.concatenate([right, jnp.concatenate(ws, axis=0).astype(BF)], axis=1)


def mix_factor(sum_refs):
    total = sum_refs[0][...]
    for ref in sum_refs[1:]:
        total = total + ref[...]
    force_sq = jnp.sum(total[0:1], axis=1, keepdims=True)
    vel_sq = jnp.sum(total[1:2], axis=1, keepdims=True)
    return jnp.sqrt(vel_sq / (force_sq + EPSILON))


def quench_update(dims, mix, x_ref, f_of, v_of, planes, x_out, v_out):
    gy, _ = dims[1:]
    for k in range(3):
        for p in range(planes):
            for y in range(gy):
                v = (1.0 - ALPHA_MIX) * v_of(k, p, y) + ALPHA_MIX * mix * f_of(k, p, y)
                if v_out is not None:
                    v_out[k, p, y] = v
                x_out[k, p, y] = x_ref[k, p, y] + STEP_SIZE * v


def density_kernel(dims, first, *refs):
    planes, gy, gz = dims
    if first:
        (p0, p1, p2, c0, c1, c2, fl, fl_lo, emb_ref, lo_ref, hi_ref, list_ref, lhs_ref, right_ref, res_ref, size_ref) = refs
        lister = ListBuilder(dims, lhs_ref.shape[-1], (c0, c1, c2), fl, fl_lo, list_ref, size_ref)
    else:
        (q0, q1, q2, c0, c1, c2, list_ref, f_ref, v_ref, b0, b2) = refs[:11]
        sum_refs = refs[11:-10]
        (emb_ref, lo_ref, hi_ref, p0, p1, p2, v_out, lhs_ref, right_ref, res_ref) = refs[-10:]
        lister = None
        mix = mix_factor(sum_refs)
        quench_update(
            dims, mix, q1, lambda k, p, y: f_ref[k, p, y], lambda k, p, y: v_ref[k, p, y], planes, p1, v_out
        )
        for q, b, out in ((q0, b0, p0), (q2, b2, p2)):
            quench_update(
                dims, mix, q, lambda k, p, y, b=b: b[k, p, y], lambda k, p, y, b=b: b[k + 3, p, y], 1, out, None
            )
    slots = lhs_ref.shape[-1]
    build_partners(dims, (p0, p1, p2), (c0, c1, c2), None, lister, lhs_ref, None)
    build_rights(dims, p1, c1, None, right_ref)
    gap = jnp.zeros((slots - KDIM, slots), BF)
    side = jnp.zeros((slots, slots), BF)

    def right_of(cell):
        one = jnp.concatenate([right_ref[cell], gap], axis=0)
        return jnp.concatenate(
            [jnp.concatenate([one, side], axis=1), jnp.concatenate([side, one], axis=1)], axis=0
        )

    def left_of(starts):
        return jnp.concatenate([lhs_ref[tile_at(start), :] for start in starts], axis=1)

    def work(starts, value, acc):
        for r in range(TILE // 8):
            for h in range(2):
                t = jnp.maximum(value[r * 8 : r * 8 + 8, h * slots : (h + 1) * slots], 0.0)
                acc[r % 4] = acc[r % 4] + t * t * t

    def emit(cell, acc):
        res_ref[cell] = (acc[0] + acc[1]) + (acc[2] + acc[3])

    run_items(dims, slots, list_ref, GROUP, 2, 4, right_of, left_of, work, emit)
    lane = lax.broadcasted_iota(jnp.int32, (1, slots), 1)
    for p in range(planes):

        def row(y, _):
            for z in range(gz):
                total = jnp.sum(res_ref[(p * gy + y) * gz + z], axis=0, keepdims=True)
                total = total - jnp.where(lane < c1[p, y, z], 1.0, 0.0)
                emb = -lax.rsqrt(1.0 + total / slots)
                emb_ref[p, y, z : z + 1, :] = emb
                if p == 0:
                    lo_ref[0, y, z : z + 1, :] = emb
                if p == planes - 1:
                    hi_ref[0, y, z : z + 1, :] = emb
            return 0

        lax.fori_loop(0, gy, row, 0)


def build_rights(dims, pos, cnt, emb, right_ref):
    planes, gy, gz = dims
    for p in range(planes):

        def row(y, _):
            for z in range(gz):
                x3 = [pos[k, p, y, z : z + 1, :] for k in range(3)]
                e_row = None if emb is None else emb[p, y, z : z + 1, :]
                right_ref[(p * gy + y) * gz + z] = build_center(
                    dims, p, y, jnp.int32(z), x3, cnt[p, y, z], e_row
                )
            return 0

        lax.fori_loop(0, gy, row, 0)


def tile_at(start):
    return pl.ds(pl.multiple_of(start, TILE), TILE)


def run_items(dims, slots, list_ref, group, width, chains, right_of, left_of, work, emit):
    head, items, _ = list_sizes(dims, slots)
    entries = head + items
    turns = ITEM // (2 * width)

    def inner(*flat):
        accs = [
            [[flat[(i * 2 + m) * turns + t] for t in range(turns)] for m in range(2)]
            for i in range(group)
        ]

        def starts_of(item, m, t):
            return [list_ref[entries + item * ITEM + (t * 2 + m) * width + w] for w in range(width)]

        def load_right(item):
            right = right_of(list_ref[head + item])
            for m in range(2):
                pltpu.matmul_push_rhs(right, staging_register=0, mxu_index=m)

        def send(item, i, m, t):
            pltpu.matmul_acc_lhs(
                accs[i][m][t],
                left_of(starts_of(item, m, t)),
                load_staged_rhs=0 if t == 0 else None,
            )

        for i in range(group):
            load_right(i)
            for t in range(turns):
                for m in range(2):
                    send(i, i, m, t)

        def step(turn, carry):
            acc = list(carry)
            for i in range(group):
                item = turn * group + i
                cell = list_ref[head + item]
                same = cell == list_ref[head + jnp.maximum(item - 1, 0)]
                keep = same.astype(F32)
                acc = [value * keep for value in acc]
                load_right(item + group)
                for t in range(turns):
                    for m in range(2):
                        value = pltpu.matmul_pop(accs[i][m][t])
                        send(item + group, i, m, t)
                        work(starts_of(item, m, t), value, acc)
                emit(cell, acc)
            return tuple(acc)

        zero = jnp.zeros((8, slots), F32)
        lax.fori_loop(0, list_ref[0] // group, step, (zero,) * chains)
        for i in range(group):
            for t in range(turns):
                for m in range(2):
                    pltpu.matmul_pop(accs[i][m][t])

    pl.run_scoped(
        inner,
        *[
            pltpu.ACC(m)((TILE, 2 * slots), F32)
            for _ in range(group)
            for m in range(2)
            for _ in range(turns)
        ],
    )


def force_kernel(dims, *refs):
    (p0, p1, p2, c0, c1, c2, e0, e1, e2, vel, list_ref) = refs[:11]
    (f_ref, v_ref, s_ref) = refs[11:14]
    edges = refs[14:-4]
    (lhs_ref, right_ref, res_ref, wide_ref) = refs[-4:]
    planes, gy, gz = dims
    slots = lhs_ref.shape[-1]
    pl.run_scoped(
        functools.partial(build_partners, dims, (p0, p1, p2), (c0, c1, c2), (e0, e1, e2), None, lhs_ref, wide_ref),
        *[pltpu.ACC(0)((slots, 2 * slots), F32) for _ in range(gz)],
        *[pltpu.ACC(1)((slots // 2, 2 * slots), F32) for _ in range(gz)],
    )
    build_rights(dims, p1, c1, e1, right_ref)
    gap = jnp.zeros((2 * slots - KDIM, 2 * slots), BF)
    side = jnp.zeros((TILE, slots), BF)

    def right_of(cell):
        return jnp.concatenate([right_ref[cell], gap], axis=0)

    def left_of(starts):
        return jnp.concatenate([lhs_ref[tile_at(starts[0]), :], side], axis=1)

    def work(starts, value, acc):
        wides = [wide_ref[k, tile_at(starts[0]), :] for k in range(3)]
        for r in range(TILE // 8):
            here = slice(r * 8, r * 8 + 8)
            t = jnp.maximum(value[here, :slots], 0.0)
            g = t * t * value[here, slots:]
            at = (r % 2) * 4
            acc[at] = acc[at] + g
            for k in range(3):
                acc[at + 1 + k] = acc[at + 1 + k] + g * wides[k][here]

    def emit(cell, acc):
        for k in range(4):
            res_ref[cell, k] = acc[k] + acc[k + 4]

    run_items(dims, slots, list_ref, 2, 1, 8, right_of, left_of, work, emit)
    lane = lax.broadcasted_iota(jnp.int32, (1, slots), 1)
    sums = (jnp.zeros((1, slots), F32), jnp.zeros((1, slots), F32))
    for p in range(planes):

        def row(y, sums):
            ff, vv = sums
            for z in range(gz):
                cell = (p * gy + y) * gz + z
                one = slice(z, z + 1)
                center = (
                    p + 0.5 - (planes + 1) / 2,
                    y.astype(F32) + 0.5 - (gy + 1) / 2,
                    z + 0.5 - (gz + 1) / 2,
                )
                total = jnp.sum(res_ref[cell, 0], axis=0, keepdims=True)
                for k in range(3):
                    x = p1[k, p, y, one, :] + center[k]
                    f = (24.0 / slots) * (x * total - jnp.sum(res_ref[cell, k + 1], axis=0, keepdims=True))
                    f_ref[k, p, y, one, :] = f
                    v = jnp.where(lane < c1[p, y, z], vel[k, p, y, one, :], 0.0) + STEP_SIZE * f
                    v_ref[k, p, y, one, :] = v
                    if edges and p == 0:
                        edges[0][k, 0, y, one, :] = f
                        edges[0][k + 3, 0, y, one, :] = v
                    if edges and p == planes - 1:
                        edges[1][k, 0, y, one, :] = f
                        edges[1][k + 3, 0, y, one, :] = v
                    ff = ff + f * f
                    vv = vv + v * v
            return ff, vv

        sums = lax.fori_loop(0, gy, row, sums)
    s_ref[...] = jnp.concatenate([sums[0], sums[1], jnp.zeros((6, slots), F32)], axis=0)


def finish_kernel(dims, radix, *refs):
    (x_ref, f_ref, v_ref, noise, cnt, pick) = refs[:6]
    options = refs[6 : 6 + radix]
    sum_refs = refs[6 + radix : -4]
    (xq, vq, xd, vd) = refs[-4:]
    planes, gy, gz = dims
    slots = x_ref.shape[-1]
    mix = mix_factor(sum_refs)
    quench_update(
        dims, mix, x_ref, lambda k, p, y: f_ref[k, p, y], lambda k, p, y: v_ref[k, p, y], planes, xq, vq
    )
    lane = lax.broadcasted_iota(jnp.int32, (gz, slots), 1)
    line = lax.broadcasted_iota(jnp.int32, (gz, slots), 0)
    take = pick[0]
    for p in range(planes):
        for y in range(gy):
            limit = jnp.zeros((gz, slots), jnp.int32)
            for z in range(gz):
                limit = jnp.where(line == z, cnt[p, y, z], limit)
            occupied = (lane < limit).astype(F32)
            for k in range(3):
                place, push = options[0][k, p, y], options[0][k + 3, p, y]
                for index in range(1, radix):
                    place = jnp.where(take == index, options[index][k, p, y], place)
                    push = jnp.where(take == index, options[index][k + 3, p, y], push)
                v = FRICTION * push + KICK_SCALE * occupied * noise[k, p, y]
                vd[k, p, y] = v
                xd[k, p, y] = place + STEP_SIZE * v


def exit_hops(count):
    hops, stride = [], 1
    while stride < count:
        left = count // stride
        radix = next(r for r in (4, 2, 3, 5, 7, left) if left % r == 0)
        hops.append((stride, radix))
        stride *= radix
    return hops


def body(positions, velocities, thermal_noise, counts, pair_flags, exit_replica):
    start_pos = positions[0]
    start_vel = velocities[0]
    planes, gy, gz, slots = start_pos.shape[1:]
    dims = (planes, gy, gz)
    up, down = ring("space", 1), ring("space", -1)
    space = lax.axis_size("space")
    vmem = pl.BlockSpec(memory_space=pltpu.VMEM)
    smem = pl.BlockSpec(memory_space=pltpu.SMEM)
    ext = (planes + 2) * (gy + 2) * (gz + 2) + 1
    cells = planes * gy * gz
    entries = list_sizes(dims, slots)[2]
    pairs = planes * gy * gz * 27 * slots * slots

    def shaped(*shape):
        return jax.ShapeDtypeStruct(shape, F32)

    def planes_of(block, dim):
        return lax.slice_in_dim(block, 0, 1, axis=dim), lax.slice_in_dim(block, planes - 1, planes, axis=dim)

    def halo(first, last):
        return lax.ppermute(last, "space", up), lax.ppermute(first, "space", down)

    flags_lo = lax.ppermute(lax.slice_in_dim(pair_flags, planes - 1, planes, axis=1), "space", up)
    count_lo, count_hi = halo(*planes_of(counts, 0))
    pos_lo, pos_hi = halo(*planes_of(start_pos, 1))
    lhs_scratch = pltpu.VMEM((ext * slots, slots), BF)
    scratch_d = [lhs_scratch, pltpu.VMEM((cells, KDIM, slots), BF), pltpu.VMEM((cells, 8, slots), F32)]
    scratch_f = [
        lhs_scratch,
        pltpu.VMEM((cells, KDIM, 2 * slots), BF),
        pltpu.VMEM((cells, 4, 8, slots), F32),
        pltpu.VMEM((3, ext * slots, slots), F32),
    ]
    emb_shape = [shaped(planes, gy, gz, slots), shaped(1, gy, gz, slots), shaped(1, gy, gz, slots)]
    vec, edge = shaped(3, planes, gy, gz, slots), shaped(3, 1, gy, gz, slots)
    pack = shaped(6, 1, gy, gz, slots)
    number = [smem] * 3
    cost_d = pl.CostEstimate(flops=pairs * 10, bytes_accessed=2**20, transcendentals=0)
    cost_f = pl.CostEstimate(flops=pairs * 25, bytes_accessed=2**20, transcendentals=0)

    held, hops = None, exit_hops(lax.axis_size("rep"))
    me, chosen = lax.axis_index("rep"), exit_replica[0]

    def hop(index, held):
        stride, radix = hops[index]
        digit, root = (me // stride) % radix, (chosen // stride) % radix
        options = [held]
        for turn in range(1, radix):
            pairs = []
            for i in range(lax.axis_size("rep")):
                at = (i // stride) % radix
                pairs.append((i, i + (((at + turn) % radix) - at) * stride))
            options.append(lax.ppermute(held, "rep", pairs))
        return options, (digit - root) % radix

    motion = start_vel
    coords = (pos_lo, start_pos, pos_hi)
    for quench_step in range(QUENCH):
        args = [*coords, count_lo, counts, count_hi]
        specs = [vmem] * 3 + number
        if quench_step == 0:
            emb, emb_first, emb_last, blocks = pl.pallas_call(
                functools.partial(density_kernel, dims, True),
                out_shape=(*emb_shape, jax.ShapeDtypeStruct((entries,), jnp.int32)),
                in_specs=specs + [smem, smem],
                out_specs=(vmem, vmem, vmem, smem),
                scratch_shapes=scratch_d + [pltpu.SMEM(((planes + 2) * gy * gz,), jnp.int32)],
                compiler_params=pltpu.CompilerParams(vmem_limit_bytes=12 * 2**20),
                cost_estimate=cost_d,
                name="density_first",
            )(*args, pair_flags, flags_lo)
        else:
            emb, emb_first, emb_last, *coords, motion = pl.pallas_call(
                functools.partial(density_kernel, dims, False),
                out_shape=(*emb_shape, edge, vec, edge, vec),
                in_specs=specs + [smem] + [vmem] * (4 + space),
                out_specs=(vmem,) * 7,
                scratch_shapes=scratch_d,
                compiler_params=pltpu.CompilerParams(vmem_limit_bytes=12 * 2**20),
                cost_estimate=cost_d,
                name="density_next",
            )(*args, blocks, forces, pushed, *packs, *sums)
            args = [*coords, count_lo, counts, count_hi]
        emb_lo, emb_hi = halo(emb_first, emb_last)
        last = quench_step == QUENCH - 1
        forces, pushed, part, *edges = pl.pallas_call(
            functools.partial(force_kernel, dims),
            out_shape=(vec, vec, shaped(8, slots), *(() if last else (pack, pack))),
            in_specs=specs + [vmem] * 4 + [smem],
            out_specs=(vmem,) * (3 if last else 5),
            scratch_shapes=scratch_f,
            compiler_params=pltpu.CompilerParams(vmem_limit_bytes=42 * 2**20),
            cost_estimate=cost_f,
            name="force",
        )(*args, emb_lo, emb, emb_hi, motion, blocks)
        sums = [part] + [lax.ppermute(part, "space", ring("space", s)) for s in range(1, space)]
        if not last:
            packs = halo(*edges)
        if quench_step == 0:
            held = jnp.concatenate([start_pos, pushed], axis=0)
            for index in range(len(hops) - 1):
                options, pick = hop(index, held)
                held = options[0]
                for turn in range(1, len(options)):
                    held = jnp.where(pick == turn, options[turn], held)
            options, pick = hop(len(hops) - 1, held)

    quench_pos, quench_vel, place, drift = pl.pallas_call(
        functools.partial(finish_kernel, dims, len(options)),
        out_shape=(vec,) * 4,
        in_specs=[vmem] * 4 + [smem] * 2 + [vmem] * (len(options) + space),
        out_specs=(vmem,) * 4,
        compiler_params=pltpu.CompilerParams(vmem_limit_bytes=12 * 2**20),
        name="finish",
    )(coords[1], forces, pushed, thermal_noise[0, 0], counts, pick[None], *options, *sums)
    return quench_pos[None], quench_vel[None], place[None], drift[None]


def solution(mesh):
    vector = P("rep", None, "space", None, None, None)
    placed = (
        vector,
        vector,
        P("rep", None, None, "space", None, None, None),
        P("space", None, None),
        P(None, "space", None, None),
        P(),
    )
    return jax.shard_map(body, mesh=mesh, in_specs=placed, out_specs=(vector,) * 4, check_vma=False)
```

```python
import functools
import math

import jax
import jax.numpy as jnp
from jax import lax
from jax.experimental import pallas as pl
from jax.experimental.pallas import tpu as pltpu
from jax.sharding import PartitionSpec as P


QUENCH = 2
STEP_SIZE = 0.1
ALPHA_MIX = 0.25
EPSILON = 1e-06
FRICTION = math.exp(-0.2)
KICK_SCALE = math.sqrt(1.0 - FRICTION * FRICTION)
HALF_OFFSETS = (
    [(1, p, q) for p in (-1, 0, 1) for q in (-1, 0, 1)]
    + [(0, 1, q) for q in (-1, 0, 1)]
    + [(0, 0, 1)]
)
OFFSETS = [(i, j, k) for i in (-1, 0, 1) for j in (-1, 0, 1) for k in (-1, 0, 1)]
FAR = 1.0e6
BF = jnp.bfloat16
F32 = jnp.float32
KDIM = 64
TILE = 32
ITEM = 10
GROUP = 4


def ring(axis, shift):
    count = lax.axis_size(axis)
    return [(i, (i + shift) % count) for i in range(count)]


def flag_of(offset):
    for index, entry in enumerate(HALF_OFFSETS):
        if entry == offset:
            return index, True
        if entry == tuple(-v for v in offset):
            return index, False
    return None


def rows_of(cell, slots):
    if isinstance(cell, int):
        return pl.ds(cell * slots, slots)
    return pl.ds(pl.multiple_of(cell * slots, slots), slots)


def split3(value):
    high = value.astype(BF).astype(F32)
    rest = value - high
    mid = rest.astype(BF).astype(F32)
    return high, mid, (rest - mid).astype(BF).astype(F32)


def wrap(index, size):
    index = jnp.where(index < 0, index + size, index)
    return jnp.where(index >= size, index - size, index)


def list_sizes(dims, slots):
    most = math.prod(dims) * -(-27 * (slots // TILE) // ITEM)
    head = 8
    return head, most + 2 * GROUP, head + (most + 2 * GROUP) * (ITEM + 1) + 2 * ITEM


class ListBuilder:
    def __init__(self, dims, slots, cnt, flags, flags_lo, list_ref, size_ref):
        self.dims, self.slots, self.flags, self.flags_lo = dims, slots, flags, flags_lo
        self.list_ref, self.size_ref = list_ref, size_ref
        planes, gy, gz = dims
        self.head, items, _ = list_sizes(dims, slots)
        self.entries = self.head + items
        self.dummy = (planes + 2) * (gy + 2) * (gz + 2) * slots
        cells = [(p, z) for p in range(planes) for z in range(gz)]
        self.shares = [cells[j :: planes + 2] for j in range(planes + 2)]
        for j in range(planes + 2):
            which, at = (0, 0) if j == 0 else ((2, 0) if j == planes + 1 else (1, j - 1))

            def row(y, _):
                for z in range(gz):
                    size_ref[(j * gy + y) * gz + z] = (cnt[which][at, y, z] + (TILE - 1)) >> (
                        TILE.bit_length() - 1
                    )
                return 0

            lax.fori_loop(0, gy, row, 0)

    def add_cell(self, p, y, z, item, base, near, spots):
        _, gy, gz = self.dims
        ey, ez = gy + 2, gz + 2
        at = self.entries + item * ITEM
        for ox, oy, oz in OFFSETS:
            first = (((p + 1 + ox) * ey + 1 + oy) * ez + (z + 1 + oz)) * self.slots
            jz = (z + oz) % gz
            number = self.size_ref[spots[oy] + ((p + 1 + ox) * gy * gz + jz)]
            for t in range(self.slots // TILE):
                self.list_ref[at + t] = base + (first + t * TILE)
            found = flag_of((ox, oy, oz))
            if found is not None:
                index, forward = found
                if forward:
                    flag = self.flags[index, p, y, z]
                elif p + ox < 0:
                    flag = self.flags_lo[index, 0, near[oy], jz]
                else:
                    flag = self.flags[index, p + ox, near[oy], jz]
                number = number * flag
            at = at + number
        for t in range(ITEM):
            self.list_ref[at + t] = self.dummy
        for t in range(-(-27 * (self.slots // TILE) // ITEM)):
            self.list_ref[self.head + item + t] = y * gz + (p * gy * gz + z)
        return lax.div(at - self.entries + (ITEM - 1), jnp.int32(ITEM))

    def add_row(self, j, y, item):
        gy, gz = self.dims[1:]
        base = y * ((gz + 2) * self.slots)
        near = {oy: wrap(y + oy, gy) for oy in (-1, 0, 1)}
        spots = {oy: near[oy] * gz for oy in (-1, 0, 1)}
        for p, z in self.shares[j]:
            item = self.add_cell(p, y, z, item, base, near, spots)
        return item

    def close(self, item):
        self.list_ref[0] = (item + (GROUP - 1)) // GROUP * GROUP
        last = self.list_ref[self.head + item - 1]

        def rest(i, _):
            self.list_ref[self.head + item + i] = last
            for t in range(ITEM):
                self.list_ref[self.entries + (item + i) * ITEM + t] = self.dummy
            return 0

        lax.fori_loop(0, 2 * GROUP - 1, rest, 0)


def build_partners(dims, pos, cnt, emb, lister, lhs_ref, wide_ref, *accs):
    planes, gy, gz = dims
    ey, ez = gy + 2, gz + 2
    slots = lhs_ref.shape[-1]
    full = (8, slots)
    rows = lax.broadcasted_iota(jnp.int32, full, 0)
    lane = lax.broadcasted_iota(jnp.int32, full, 1)
    blank = jnp.zeros((slots - KDIM, slots), F32)

    def store(ext, value):
        h, m, l = split3(value)
        tall = jnp.concatenate([h, h, h, m, m, m, l, l, blank], axis=0).T.astype(BF)
        lhs_ref[rows_of(ext, slots), :] = tall
        return tall

    if wide_ref is not None:
        row = lax.broadcasted_iota(jnp.int32, (2 * slots, 2 * slots), 0)
        col = lax.broadcasted_iota(jnp.int32, (2 * slots, 2 * slots), 1) // slots
        line_row = row % slots
        used = (line_row < 8) | ((line_row >= 24) & (line_row < 32)) | ((line_row >= 48) & (line_row < 56))
        side = jnp.zeros((slots, slots), BF)
        half = slots // 2
        acc_xy, acc_z = accs[:gz], accs[gz:]
        for m in range(2):
            if m == 0:
                chosen = used & (row < slots) & (line_row % 8 == col)
            else:
                chosen = used & (row // slots == col) & (line_row % 8 == 2)
            pick = jnp.where(chosen, 1.0, 0.0)
            pltpu.matmul_push_rhs(pick.astype(BF), staging_register=0, mxu_index=m)
        for acc, height in ((acc_xy[0], slots), (acc_z[0], half)):
            pltpu.matmul_acc_lhs(acc, jnp.zeros((height, 2 * slots), BF), load_staged_rhs=0)
            pltpu.matmul_pop(acc)

    def one(j, which, at, y, z, by, bz):
        raw = [
            jnp.broadcast_to(pos[which][k, at, by, pl.ds(bz, 1), :], full) for k in range(3)
        ]
        xx = raw[0] + (j - 0.5 - (planes + 1) / 2)
        yy = raw[1] + (jnp.asarray(y).astype(F32) - 0.5 - (gy + 1) / 2)
        zz = raw[2] + (z - 0.5 - (gz + 1) / 2)
        norm = xx * xx + yy * yy + zz * zz
        norm = jnp.where(lane < cnt[which][at, by, bz], norm, norm + FAR)
        value = jnp.where(rows == 0, xx, jnp.where(rows == 1, yy, zz))
        value = jnp.where(rows == 3, norm, value)
        value = jnp.where(rows >= 4, 1.0, value)
        if emb is not None:
            e = jnp.broadcast_to(emb[which][at, by, pl.ds(bz, 1), :], full) * 0.25
            value = jnp.where(rows == 6, e, value)
        return store((j * ey + y) * ez + z, value)

    def put(spot, images=()):
        for z in range(1, gz + 1):
            both = pltpu.matmul_pop(acc_xy[z - 1])
            deep = pltpu.matmul_pop(acc_z[z - 1])
            deep = jnp.concatenate([deep[:, :slots], deep[:, slots:]], axis=0)
            wide_x, wide_y = both[:, :slots], both[:, slots:]
            for line, shift in ((spot, 0.0), *images):
                here = wide_y + shift if shift else wide_y
                for at, turn in [(z, 0.0)] + [(0, -1.0 * gz)] * (z == gz) + [(gz + 1, 1.0 * gz)] * (z == 1):
                    rows_at = rows_of(line + at, slots)
                    wide_ref[0, rows_at, :] = wide_x
                    wide_ref[1, rows_at, :] = here
                    wide_ref[2, rows_at, :] = deep + turn if turn else deep

    def send(talls):
        for z in range(1, gz + 1):
            pltpu.matmul_acc_lhs(acc_xy[z - 1], jnp.concatenate([talls[z], side], axis=1))
            pltpu.matmul_acc_lhs(acc_z[z - 1], jnp.concatenate([talls[z][:half], talls[z][half:]], axis=1))

    item = jnp.int32(0)
    for j in range(planes + 2):
        which, at = (0, 0) if j == 0 else ((2, 0) if j == planes + 1 else (1, j - 1))

        def line(y, by):
            return [one(j, which, at, y, z, by, (z - 1) % gz) for z in range(ez)]

        def wide_line(y):
            talls = line(y, y - 1)
            put((j * ey + y - 1) * ez)
            send(talls)
            return 0

        def line_and_list(y, item):
            line(y, wrap(y - 1, gy))
            return lister.add_row(j, y, item)

        def plain(y, _):
            line(y, wrap(y - 1, gy))
            return 0

        if wide_ref is not None:
            base = j * ey * ez
            line(0, gy - 1)
            send(line(1, 0))
            talls = line(2, 1)
            put(base + ez, [(base + (gy + 1) * ez, 1.0 * gy)])
            send(talls)
            for y in range(3, gy + 1):
                wide_line(y)
            line(gy + 1, 0)
            put(base + gy * ez, [(base, -1.0 * gy)])
        elif lister is None:
            lax.fori_loop(0, ey, plain, 0, unroll=3)
        else:
            item = lax.fori_loop(0, gy, line_and_list, item)
            lax.fori_loop(gy, ey, plain, 0, unroll=2)
    if lister is not None:
        lister.close(item)
    if wide_ref is not None:
        for k in range(3):
            wide_ref[k, (planes + 2) * ey * ez * slots :, :] = jnp.zeros((slots, slots), F32)
    store((planes + 2) * ey * ez, jnp.where(rows == 3, FAR, jnp.where(rows >= 4, 1.0, 0.0)))


def build_center(dims, p, y, z, x3, count, e_row):
    planes, gy, gz = dims
    slots = x3[0].shape[-1]
    full = (8, slots)
    rows = lax.broadcasted_iota(jnp.int32, full, 0)
    lane = lax.broadcasted_iota(jnp.int32, full, 1)
    xx = jnp.broadcast_to(x3[0], full) + (p + 0.5 - (planes + 1) / 2)
    yy = jnp.broadcast_to(x3[1], full) + (y.astype(F32) + 0.5 - (gy + 1) / 2)
    zz = jnp.broadcast_to(x3[2], full) + (z.astype(F32) + 0.5 - (gz + 1) / 2)
    one = 1.0 - (xx * xx + yy * yy + zz * zz)
    one = jnp.where(lane < count, one, one - FAR)
    value = jnp.where(rows == 0, xx, jnp.where(rows == 1, yy, zz)) * 2.0
    value = jnp.where(rows == 4, one, value)
    if e_row is not None:
        value = jnp.where(rows == 5, jnp.broadcast_to(e_row, full) * 0.25, value)
    parts = split3(value)
    us, ws = [], []
    for block in range(8):
        part = parts[block % 3]
        keep = rows < 3
        if block < 3:
            keep = keep | (rows == 4)
        u = jnp.where(keep, part, 0.0)
        if block % 3 == 0:
            u = jnp.where(rows == 3, -1.0, u)
        us.append(u)
        if e_row is not None:
            w = u
            if block < 3:
                w = jnp.where(rows == 5, part, w)
            if block % 3 == 0:
                w = jnp.where(rows == 6, 1.0, w)
            ws.append(w)
    right = jnp.concatenate(us, axis=0).astype(BF)
    if e_row is None:
        return right
    return jnp.concatenate([right, jnp.concatenate(ws, axis=0).astype(BF)], axis=1)


def mix_factor(sum_refs):
    total = sum_refs[0][...]
    for ref in sum_refs[1:]:
        total = total + ref[...]
    force_sq = jnp.sum(total[0:1], axis=1, keepdims=True)
    vel_sq = jnp.sum(total[1:2], axis=1, keepdims=True)
    return jnp.sqrt(vel_sq / (force_sq + EPSILON))


def quench_update(dims, mix, x_ref, f_of, v_of, planes, x_out, v_out):
    gy, _ = dims[1:]
    for k in range(3):
        for p in range(planes):
            for y in range(gy):
                v = (1.0 - ALPHA_MIX) * v_of(k, p, y) + ALPHA_MIX * mix * f_of(k, p, y)
                if v_out is not None:
                    v_out[k, p, y] = v
                x_out[k, p, y] = x_ref[k, p, y] + STEP_SIZE * v


def density_kernel(dims, first, *refs):
    planes, gy, gz = dims
    if first:
        (p0, p1, p2, c0, c1, c2, fl, fl_lo, emb_ref, lo_ref, hi_ref, list_ref, lhs_ref, right_ref, res_ref, size_ref) = refs
        lister = ListBuilder(dims, lhs_ref.shape[-1], (c0, c1, c2), fl, fl_lo, list_ref, size_ref)
    else:
        (q0, q1, q2, c0, c1, c2, list_ref, f_ref, v_ref, b0, b2) = refs[:11]
        sum_refs = refs[11:-10]
        (emb_ref, lo_ref, hi_ref, p0, p1, p2, v_out, lhs_ref, right_ref, res_ref) = refs[-10:]
        lister = None
        mix = mix_factor(sum_refs)
        quench_update(
            dims, mix, q1, lambda k, p, y: f_ref[k, p, y], lambda k, p, y: v_ref[k, p, y], planes, p1, v_out
        )
        for q, b, out in ((q0, b0, p0), (q2, b2, p2)):
            quench_update(
                dims, mix, q, lambda k, p, y, b=b: b[k, p, y], lambda k, p, y, b=b: b[k + 3, p, y], 1, out, None
            )
    slots = lhs_ref.shape[-1]
    build_partners(dims, (p0, p1, p2), (c0, c1, c2), None, lister, lhs_ref, None)
    build_rights(dims, p1, c1, None, right_ref)
    gap = jnp.zeros((slots - KDIM, slots), BF)
    side = jnp.zeros((slots, slots), BF)

    def right_of(cell):
        one = jnp.concatenate([right_ref[cell], gap], axis=0)
        return jnp.concatenate(
            [jnp.concatenate([one, side], axis=1), jnp.concatenate([side, one], axis=1)], axis=0
        )

    def left_of(starts):
        return jnp.concatenate([lhs_ref[tile_at(start), :] for start in starts], axis=1)

    def work(starts, value, acc):
        for r in range(TILE // 8):
            for h in range(2):
                t = jnp.maximum(value[r * 8 : r * 8 + 8, h * slots : (h + 1) * slots], 0.0)
                acc[r % 2] = acc[r % 2] + t * t * t

    def emit(cell, acc):
        res_ref[cell] = acc[0] + acc[1]

    run_items(dims, slots, list_ref, GROUP, 2, 2, right_of, left_of, work, emit)
    lane = lax.broadcasted_iota(jnp.int32, (1, slots), 1)
    for p in range(planes):

        def row(y):
            for z in range(gz):
                total = jnp.sum(res_ref[(p * gy + y) * gz + z], axis=0, keepdims=True)
                total = total - jnp.where(lane < c1[p, y, z], 1.0, 0.0)
                emb = -lax.rsqrt(1.0 + total / slots)
                emb_ref[p, y, z : z + 1, :] = emb
                if p == 0:
                    lo_ref[0, y, z : z + 1, :] = emb
                if p == planes - 1:
                    hi_ref[0, y, z : z + 1, :] = emb
            return 0

        for y in range(gy):
            row(y)


def build_rights(dims, pos, cnt, emb, right_ref):
    planes, gy, gz = dims
    for p in range(planes):

        def row(y, _):
            for z in range(gz):
                x3 = [pos[k, p, y, z : z + 1, :] for k in range(3)]
                e_row = None if emb is None else emb[p, y, z : z + 1, :]
                right_ref[(p * gy + y) * gz + z] = build_center(
                    dims, p, y, jnp.int32(z), x3, cnt[p, y, z], e_row
                )
            return 0

        lax.fori_loop(0, gy, row, 0)


def tile_at(start):
    return pl.ds(pl.multiple_of(start, TILE), TILE)


def run_items(dims, slots, list_ref, group, width, chains, right_of, left_of, work, emit):
    head, items, _ = list_sizes(dims, slots)
    entries = head + items
    turns = ITEM // width

    def inner(*flat):
        accs = [flat[i * turns : (i + 1) * turns] for i in range(group)]

        def starts_of(item, t):
            return [list_ref[entries + item * ITEM + t * width + w] for w in range(width)]

        def load_right(item, i):
            right = right_of(list_ref[head + item])
            pltpu.matmul_push_rhs(right, staging_register=0, mxu_index=i % 2)

        def send(item, i, t):
            pltpu.matmul_acc_lhs(
                accs[i][t], left_of(starts_of(item, t)), load_staged_rhs=0 if t == 0 else None
            )

        for i in range(group):
            load_right(i, i)
            for t in range(turns):
                send(i, i, t)

        def step(turn, carry):
            acc = list(carry)
            for pair in range(0, group, 2):
                items = [turn * group + pair + i for i in range(2)]
                cells = [list_ref[head + item] for item in items]
                before = list_ref[head + jnp.maximum(items[0] - 1, 0)]
                same = [cells[0] == before, cells[1] == cells[0]]
                keep = same[0].astype(F32)
                both = [[value * keep for value in acc], [jnp.zeros((8, slots), F32)] * chains]
                for i in range(2):
                    load_right(items[i] + group, pair + i)
                for t in range(turns):
                    for i in range(2):
                        value = pltpu.matmul_pop(accs[pair + i][t])
                        send(items[i] + group, pair + i, t)
                        work(starts_of(items[i], t), value, both[i])
                emit(cells[0], both[0])
                keep = same[1].astype(F32)
                acc = [second + first * keep for first, second in zip(*both)]
                emit(cells[1], acc)
            return tuple(acc)

        zero = jnp.zeros((8, slots), F32)
        lax.fori_loop(0, list_ref[0] // group, step, (zero,) * chains)
        for i in range(group):
            for t in range(turns):
                pltpu.matmul_pop(accs[i][t])

    pl.run_scoped(
        inner,
        *[
            pltpu.ACC(i % 2)((TILE, 2 * slots), F32)
            for i in range(group)
            for _ in range(turns)
        ],
    )


def force_kernel(dims, *refs):
    (p0, p1, p2, c0, c1, c2, e0, e1, e2, vel, list_ref) = refs[:11]
    (f_ref, v_ref, s_ref) = refs[11:14]
    edges = refs[14:-4]
    (lhs_ref, right_ref, res_ref, wide_ref) = refs[-4:]
    planes, gy, gz = dims
    slots = lhs_ref.shape[-1]
    pl.run_scoped(
        functools.partial(build_partners, dims, (p0, p1, p2), (c0, c1, c2), (e0, e1, e2), None, lhs_ref, wide_ref),
        *[pltpu.ACC(0)((slots, 2 * slots), F32) for _ in range(gz)],
        *[pltpu.ACC(1)((slots // 2, 2 * slots), F32) for _ in range(gz)],
    )
    build_rights(dims, p1, c1, e1, right_ref)
    gap = jnp.zeros((2 * slots - KDIM, 2 * slots), BF)
    side = jnp.zeros((TILE, slots), BF)

    def right_of(cell):
        return jnp.concatenate([right_ref[cell], gap], axis=0)

    def left_of(starts):
        return jnp.concatenate([lhs_ref[tile_at(starts[0]), :], side], axis=1)

    def work(starts, value, acc):
        wides = [wide_ref[k, tile_at(starts[0]), :] for k in range(3)]
        for r in range(TILE // 8):
            here = slice(r * 8, r * 8 + 8)
            t = jnp.maximum(value[here, :slots], 0.0)
            g = t * t * value[here, slots:]
            acc[0] = acc[0] + g
            for k in range(3):
                acc[1 + k] = acc[1 + k] + g * wides[k][here]

    def emit(cell, acc):
        for k in range(4):
            res_ref[cell, k] = acc[k]

    run_items(dims, slots, list_ref, 2, 1, 4, right_of, left_of, work, emit)
    lane = lax.broadcasted_iota(jnp.int32, (1, slots), 1)
    sums = (jnp.zeros((1, slots), F32), jnp.zeros((1, slots), F32))
    for p in range(planes):

        def row(y, sums):
            ff, vv = sums
            for z in range(gz):
                cell = (p * gy + y) * gz + z
                one = slice(z, z + 1)
                center = (
                    p + 0.5 - (planes + 1) / 2,
                    y + 0.5 - (gy + 1) / 2,
                    z + 0.5 - (gz + 1) / 2,
                )
                total = jnp.sum(res_ref[cell, 0], axis=0, keepdims=True)
                for k in range(3):
                    x = p1[k, p, y, one, :] + center[k]
                    f = (24.0 / slots) * (x * total - jnp.sum(res_ref[cell, k + 1], axis=0, keepdims=True))
                    f_ref[k, p, y, one, :] = f
                    v = jnp.where(lane < c1[p, y, z], vel[k, p, y, one, :], 0.0) + STEP_SIZE * f
                    v_ref[k, p, y, one, :] = v
                    if edges and p == 0:
                        edges[0][k, 0, y, one, :] = f
                        edges[0][k + 3, 0, y, one, :] = v
                    if edges and p == planes - 1:
                        edges[1][k, 0, y, one, :] = f
                        edges[1][k + 3, 0, y, one, :] = v
                    ff = ff + f * f
                    vv = vv + v * v
            return ff, vv

        for y in range(gy):
            sums = row(y, sums)
    s_ref[...] = jnp.concatenate([sums[0], sums[1], jnp.zeros((6, slots), F32)], axis=0)


def finish_kernel(dims, radix, *refs):
    (x_ref, f_ref, v_ref, noise, cnt, pick) = refs[:6]
    options = refs[6 : 6 + radix]
    sum_refs = refs[6 + radix : -4]
    (xq, vq, xd, vd) = refs[-4:]
    planes, gy, gz = dims
    slots = x_ref.shape[-1]
    mix = mix_factor(sum_refs)
    quench_update(
        dims, mix, x_ref, lambda k, p, y: f_ref[k, p, y], lambda k, p, y: v_ref[k, p, y], planes, xq, vq
    )
    lane = lax.broadcasted_iota(jnp.int32, (gz, slots), 1)
    line = lax.broadcasted_iota(jnp.int32, (gz, slots), 0)
    take = pick[0]
    for p in range(planes):
        for y in range(gy):
            limit = jnp.zeros((gz, slots), jnp.int32)
            for z in range(gz):
                limit = jnp.where(line == z, cnt[p, y, z], limit)
            occupied = (lane < limit).astype(F32)
            for k in range(3):
                place, push = options[0][k, p, y], options[0][k + 3, p, y]
                for index in range(1, radix):
                    place = jnp.where(take == index, options[index][k, p, y], place)
                    push = jnp.where(take == index, options[index][k + 3, p, y], push)
                v = FRICTION * push + KICK_SCALE * occupied * noise[k, p, y]
                vd[k, p, y] = v
                xd[k, p, y] = place + STEP_SIZE * v


def exit_hops(count):
    hops, stride = [], 1
    while stride < count:
        left = count // stride
        radix = next(r for r in (4, 2, 3, 5, 7, left) if left % r == 0)
        hops.append((stride, radix))
        stride *= radix
    return hops


def body(positions, velocities, thermal_noise, counts, pair_flags, exit_replica):
    start_pos = positions[0]
    start_vel = velocities[0]
    planes, gy, gz, slots = start_pos.shape[1:]
    dims = (planes, gy, gz)
    up, down = ring("space", 1), ring("space", -1)
    space = lax.axis_size("space")
    vmem = pl.BlockSpec(memory_space=pltpu.VMEM)
    smem = pl.BlockSpec(memory_space=pltpu.SMEM)
    ext = (planes + 2) * (gy + 2) * (gz + 2) + 1
    cells = planes * gy * gz
    entries = list_sizes(dims, slots)[2]
    pairs = planes * gy * gz * 27 * slots * slots

    def shaped(*shape):
        return jax.ShapeDtypeStruct(shape, F32)

    def planes_of(block, dim):
        return lax.slice_in_dim(block, 0, 1, axis=dim), lax.slice_in_dim(block, planes - 1, planes, axis=dim)

    def halo(first, last):
        return lax.ppermute(last, "space", up), lax.ppermute(first, "space", down)

    flags_lo = lax.ppermute(lax.slice_in_dim(pair_flags, planes - 1, planes, axis=1), "space", up)
    count_lo, count_hi = halo(*planes_of(counts, 0))
    pos_lo, pos_hi = halo(*planes_of(start_pos, 1))
    lhs_scratch = pltpu.VMEM((ext * slots, slots), BF)
    scratch_d = [lhs_scratch, pltpu.VMEM((cells, KDIM, slots), BF), pltpu.VMEM((cells, 8, slots), F32)]
    scratch_f = [
        lhs_scratch,
        pltpu.VMEM((cells, KDIM, 2 * slots), BF),
        pltpu.VMEM((cells, 4, 8, slots), F32),
        pltpu.VMEM((3, ext * slots, slots), F32),
    ]
    emb_shape = [shaped(planes, gy, gz, slots), shaped(1, gy, gz, slots), shaped(1, gy, gz, slots)]
    vec, edge = shaped(3, planes, gy, gz, slots), shaped(3, 1, gy, gz, slots)
    pack = shaped(6, 1, gy, gz, slots)
    number = [smem] * 3
    cost_d = pl.CostEstimate(flops=pairs * 10, bytes_accessed=2**20, transcendentals=0)
    cost_f = pl.CostEstimate(flops=pairs * 25, bytes_accessed=2**20, transcendentals=0)

    held, hops = None, exit_hops(lax.axis_size("rep"))
    me, chosen = lax.axis_index("rep"), exit_replica[0]

    def hop(index, held):
        stride, radix = hops[index]
        digit, root = (me // stride) % radix, (chosen // stride) % radix
        options = [held]
        for turn in range(1, radix):
            pairs = []
            for i in range(lax.axis_size("rep")):
                at = (i // stride) % radix
                pairs.append((i, i + (((at + turn) % radix) - at) * stride))
            options.append(lax.ppermute(held, "rep", pairs))
        return options, (digit - root) % radix

    motion = start_vel
    coords = (pos_lo, start_pos, pos_hi)
    for quench_step in range(QUENCH):
        args = [*coords, count_lo, counts, count_hi]
        specs = [vmem] * 3 + number
        if quench_step == 0:
            emb, emb_first, emb_last, blocks = pl.pallas_call(
                functools.partial(density_kernel, dims, True),
                out_shape=(*emb_shape, jax.ShapeDtypeStruct((entries,), jnp.int32)),
                in_specs=specs + [smem, smem],
                out_specs=(vmem, vmem, vmem, smem),
                scratch_shapes=scratch_d + [pltpu.SMEM(((planes + 2) * gy * gz,), jnp.int32)],
                compiler_params=pltpu.CompilerParams(vmem_limit_bytes=12 * 2**20),
                cost_estimate=cost_d,
                name="density_first",
            )(*args, pair_flags, flags_lo)
        else:
            emb, emb_first, emb_last, *coords, motion = pl.pallas_call(
                functools.partial(density_kernel, dims, False),
                out_shape=(*emb_shape, edge, vec, edge, vec),
                in_specs=specs + [smem] + [vmem] * (4 + space),
                out_specs=(vmem,) * 7,
                scratch_shapes=scratch_d,
                compiler_params=pltpu.CompilerParams(vmem_limit_bytes=12 * 2**20),
                cost_estimate=cost_d,
                name="density_next",
            )(*args, blocks, forces, pushed, *packs, *sums)
            args = [*coords, count_lo, counts, count_hi]
        emb_lo, emb_hi = halo(emb_first, emb_last)
        last = quench_step == QUENCH - 1
        forces, pushed, part, *edges = pl.pallas_call(
            functools.partial(force_kernel, dims),
            out_shape=(vec, vec, shaped(8, slots), *(() if last else (pack, pack))),
            in_specs=specs + [vmem] * 4 + [smem],
            out_specs=(vmem,) * (3 if last else 5),
            scratch_shapes=scratch_f,
            compiler_params=pltpu.CompilerParams(vmem_limit_bytes=42 * 2**20),
            cost_estimate=cost_f,
            name="force",
        )(*args, emb_lo, emb, emb_hi, motion, blocks)
        sums = [part] + [lax.ppermute(part, "space", ring("space", s)) for s in range(1, space)]
        if not last:
            packs = halo(*edges)
        if quench_step == 0:
            held = jnp.concatenate([start_pos, pushed], axis=0)
            for index in range(len(hops) - 1):
                options, pick = hop(index, held)
                held = options[0]
                for turn in range(1, len(options)):
                    held = jnp.where(pick == turn, options[turn], held)
            options, pick = hop(len(hops) - 1, held)

    quench_pos, quench_vel, place, drift = pl.pallas_call(
        functools.partial(finish_kernel, dims, len(options)),
        out_shape=(vec,) * 4,
        in_specs=[vmem] * 4 + [smem] * 2 + [vmem] * (len(options) + space),
        out_specs=(vmem,) * 4,
        compiler_params=pltpu.CompilerParams(vmem_limit_bytes=12 * 2**20),
        name="finish",
    )(coords[1], forces, pushed, thermal_noise[0, 0], counts, pick[None], *options, *sums)
    return quench_pos[None], quench_vel[None], place[None], drift[None]


def solution(mesh):
    vector = P("rep", None, "space", None, None, None)
    placed = (
        vector,
        vector,
        P("rep", None, None, "space", None, None, None),
        P("space", None, None),
        P(None, "space", None, None),
        P(),
    )
    return jax.shard_map(body, mesh=mesh, in_specs=placed, out_specs=(vector,) * 4, check_vma=False)
```
